32 devices in a mesh: dom: 8 (over z, x), line: 4 (over y, core).
Axes of the slice: x: 2, y: 2, z: 4, core: 2. Of those that a mesh axis runs over, the one named last changes fastest.
Arguments:
- right_side: float32 [64, 4096], P(None, ('dom', 'line')), may hold values from -18 to 18
- diag_blocks: bfloat16 [64, 64, 4096], P(None, None, ('dom', 'line')), may hold values from -0.5 to 3.5
- lower_blocks: bfloat16 [64, 64, 4096], P(None, None, ('dom', 'line')), may hold values from -0.375 to 0.375
- upper_blocks: bfloat16 [64, 64, 4096], P(None, None, ('dom', 'line')), may hold values from -0.375 to 0.375
- face_blocks: bfloat16 [4, 64, 64, 4096], P(None, None, None, ('dom', 'line')), may hold values from -0.75 to 0.75
- face_nbr: int32 [4, 4096], P(None, ('dom', 'line')), may hold values from 0 to 160, as said below
- send_list: int32 [2, 512], P(None, ('dom', 'line')), may hold values from 0 to 127
- inv_blocks: bfloat16 [64, 64, 4096], P(None, None, ('dom', 'line')), may hold values from -0.75 to 0.75
- fwd_blocks: bfloat16 [64, 64, 4096], P(None, None, ('dom', 'line')), may hold values from -0.625 to 0.625
- bwd_blocks: bfloat16 [64, 64, 4096], P(None, None, ('dom', 'line')), may hold values from -0.625 to 0.625
Outputs:
- update: float32 [64, 4096], P(None, ('dom', 'line'))
- hessenberg: float32 [4, 3], replicated
The draws below stay inside these ranges and needn't reach their ends.
Inputs may be any that keep to these rules, and one draw needn't show every extreme that they name: `face_nbr`: slots 128 to 159 name values received from the neighbouring partitions and slot 160 is the zero slot.
All inputs are finite; a program needn't handle non-finite values.
Results may differ from the reference program's by a relative error of at most 0.015.
Values may be sent and summed in bfloat16 or wider, within the bound.
No kernel may reach another device: no remote copies, remote signals or barrier semaphores. Data moves between devices by JAX's collectives and lax.ppermute only.
A program may use at most 64 MiB of HBM per device.

```python
import jax
import jax.numpy as jnp
from jax import lax

B = 64
LLEN = 32
FACES = 4
HALO = 16
ITERS = 3
LINES_DEV = 16
ELOC = 128
ELEMS = 4096
N_DOM = 8
N_LINE = 4


def draw_right_side(key, part):
    spread = jnp.arange(ELEMS, dtype=jnp.float32) / ELEMS
    scale = 1.0 + 2.0 * spread
    jitter = jnp.clip(jax.random.normal(key, (B, ELEMS), jnp.float32), -6.0, 6.0)
    return (jitter * scale[None, :]).astype(jnp.float32)


def draw_diag_blocks(key, part):
    first_key, second_key = jax.random.split(jax.random.fold_in(key, 11))
    leading = jax.random.uniform(first_key, (B, ELEMS), jnp.float32, 1.5, 3.0)
    jitter = jnp.clip(0.125 * jax.random.normal(second_key, (B, B, ELEMS), jnp.float32), -0.5, 0.5)
    blocks = jitter + jnp.eye(B, dtype=jnp.float32)[:, :, None] * leading[:, None, :]
    return blocks.astype(jnp.bfloat16)


def draw_face_nbr(key, part):
    base_key = jax.random.fold_in(key, 23)
    left_key = jax.random.fold_in(base_key, 0)
    right_key = jax.random.fold_in(base_key, 1)
    pick_key = jax.random.fold_in(base_key, 2)
    rest_key = jax.random.fold_in(base_key, 4)
    from_left = ELOC + jax.random.randint(left_key, (ELEMS,), 0, HALO)
    from_right = ELOC + HALO + jax.random.randint(right_key, (ELEMS,), 0, HALO)
    either_side = ELOC + jax.random.randint(pick_key, (ELEMS,), 0, 2 * HALO)
    rows = [from_left, from_right, either_side]
    for face in range(3, FACES):
        rows.append(jax.random.randint(jax.random.fold_in(rest_key, face), (ELEMS,), 0, ELOC + 2 * HALO + 1))
    table = jnp.stack(rows[:FACES], axis=0).astype(jnp.int32)
    table = table.at[FACES - 1, 0].set(ELOC + 2 * HALO)
    return table.astype(jnp.int32)


def plant(entries, key, smallest, largest):
    longest = entries.shape.index(max(entries.shape))
    spots = []
    for shift in (0, 1):
        where = [jax.random.randint(jax.random.fold_in(key, axis), (), 0, length) for axis, length in enumerate(entries.shape)]
        where[longest] = (where[longest] + shift) % entries.shape[longest]
        spots.append(tuple(where))
    return entries.at[spots[0]].set(smallest).at[spots[1]].set(largest)


def block_levels(rng, dims, pieces, smallest, top_value):
    def one(axis_at, blocks):
        steps = jax.random.uniform(jax.random.fold_in(jax.random.fold_in(rng, 6), axis_at), (blocks,), jnp.float32, smallest / len(pieces), top_value / len(pieces))
        return jnp.repeat(jnp.exp(steps), dims[axis_at] // blocks).reshape((-1,) + (1,) * (len(dims) - axis_at - 1))

    gain = one(*pieces[0])
    for cut in pieces[1:]:
        gain = gain * one(*cut)
    return gain


def normal_values(stream_key, shape, scale, most, cuts=(), kind=jnp.bfloat16):
    loudness = block_levels(stream_key, shape, cuts, -0.22, 0.18) if cuts else 1.0
    entries = jax.random.normal(stream_key, shape, jnp.float32) * scale * loudness
    return jnp.minimum(jnp.maximum(entries, -most), most).astype(kind)


def setup_inputs(seed: int = 0) -> dict:
    splits = jax.random.split(jax.random.key(seed), 11)
    return {
        "right_side": draw_right_side(jax.random.fold_in(splits[10], 71), 0),
        "diag_blocks": draw_diag_blocks(jax.random.fold_in(splits[10], 71), 0),
        "lower_blocks": normal_values(splits[2], (B, B, ELEMS), (4 * B) ** -0.5, 0.375, ((2, 32),)),
        "upper_blocks": normal_values(splits[3], (B, B, ELEMS), (4 * B) ** -0.5, 0.375, ((2, 32),)),
        "face_blocks": normal_values(splits[4], (FACES, B, B, ELEMS), B ** -0.5, 0.75, ((3, 32),)),
        "face_nbr": draw_face_nbr(jax.random.fold_in(splits[10], 71), 0),
        "send_list": plant(jax.random.randint(splits[6], (2, HALO * N_DOM * N_LINE), 0, ELOC), jax.random.fold_in(splits[6], 1), 0, ELOC - 1).astype(jnp.int32),
        "inv_blocks": normal_values(splits[7], (B, B, ELEMS), B ** -0.5, 0.75, ((2, 32),)),
        "fwd_blocks": normal_values(splits[8], (B, B, ELEMS), (B * 7 // 5) ** -0.5, 0.625, ((2, 32),)),
        "bwd_blocks": normal_values(splits[9], (B, B, ELEMS), (B * 7 // 5) ** -0.5, 0.625, ((2, 32),)),
    }


HIGHEST = lax.Precision.HIGHEST

def apply_blocks(blocks, rounded):
    return jnp.einsum('ije,je->ie', blocks.astype(jnp.float32), rounded.astype(jnp.float32), precision=HIGHEST)

def couple(blocks, carried):
    return jnp.einsum('ijnl,jnl->inl', blocks.astype(jnp.float32), carried, precision=HIGHEST)

def operate(vector, diag_blocks, lower_blocks, upper_blocks, face_blocks, face_nbr, send_list):
    rounded = vector.astype(jnp.bfloat16)
    summed = apply_blocks(diag_blocks, rounded)
    gridded = rounded.reshape(B, N_DOM, LLEN, LINES_DEV)
    earlier = jnp.pad(gridded, ((0, 0), (0, 0), (1, 0), (0, 0)))[:, :, :-1]
    following = jnp.pad(gridded, ((0, 0), (0, 0), (0, 1), (0, 0)))[:, :, 1:]
    summed = summed + apply_blocks(lower_blocks, earlier.reshape(B, ELEMS))
    summed = summed + apply_blocks(upper_blocks, following.reshape(B, ELEMS))
    partition = rounded.reshape(B, N_DOM, N_LINE, ELOC)
    sending = send_list.reshape(2, N_DOM, N_LINE, HALO)
    to_right = jnp.take_along_axis(partition, sending[0][None], axis=3)
    to_left = jnp.take_along_axis(partition, sending[1][None], axis=3)
    from_left = jnp.pad(to_right, ((0, 0), (1, 0), (0, 0), (0, 0)))[:, :-1]
    from_right = jnp.pad(to_left, ((0, 0), (0, 1), (0, 0), (0, 0)))[:, 1:]
    empty_slot = jnp.zeros((B, N_DOM, N_LINE, 1), jnp.bfloat16)
    extended = jnp.concatenate([partition, from_left, from_right, empty_slot], axis=3)
    slots = face_nbr.reshape(FACES, N_DOM, N_LINE, ELOC)
    for face in range(FACES):
        picked = jnp.take_along_axis(extended, slots[face][None], axis=3)
        summed = summed + apply_blocks(face_blocks[face], picked.reshape(B, ELEMS))
    return summed

def precondition(vector, inv_blocks, fwd_blocks, bwd_blocks):
    source = apply_blocks(inv_blocks, vector.astype(jnp.bfloat16)).reshape(B, N_DOM, LLEN, LINES_DEV)
    forward_couple = fwd_blocks.reshape(B, B, N_DOM, LLEN, LINES_DEV)
    backward_couple = bwd_blocks.reshape(B, B, N_DOM, LLEN, LINES_DEV)
    carried = jnp.zeros((B, N_DOM, LINES_DEV), jnp.float32)
    forward = []
    for position in range(LLEN):
        carried = source[:, :, position] - couple(forward_couple[:, :, :, position], carried)
        forward.append(carried)
    carried = jnp.zeros((B, N_DOM, LINES_DEV), jnp.float32)
    backward = [None] * LLEN
    for position in reversed(range(LLEN)):
        carried = forward[position] - couple(backward_couple[:, :, :, position], carried)
        backward[position] = carried
    return jnp.stack(backward, axis=2).reshape(B, ELEMS)

def reference(right_side, diag_blocks, lower_blocks, upper_blocks, face_blocks, face_nbr, send_list, inv_blocks, fwd_blocks, bwd_blocks):
    start_norm = jnp.sqrt(jnp.sum(right_side * right_side))
    krylov = [right_side / start_norm]
    search = []
    hessenberg = jnp.zeros((ITERS + 1, ITERS), jnp.float32)
    for iteration in range(ITERS):
        direction = precondition(krylov[iteration], inv_blocks, fwd_blocks, bwd_blocks)
        search.append(direction)
        product_vec = operate(direction, diag_blocks, lower_blocks, upper_blocks, face_blocks, face_nbr, send_list)
        for column in range(iteration + 1):
            weight_ij = jnp.sum(product_vec * krylov[column])
            product_vec = product_vec - weight_ij * krylov[column]
            hessenberg = hessenberg.at[column, iteration].set(weight_ij)
        height = jnp.sqrt(jnp.sum(product_vec * product_vec))
        hessenberg = hessenberg.at[iteration + 1, iteration].set(height)
        if iteration + 1 < ITERS:
            krylov.append(product_vec / height)
    normal = jnp.dot(hessenberg.T, hessenberg, precision=HIGHEST)
    target = start_norm * hessenberg[0]
    factor = jnp.linalg.cholesky(normal)
    coeffs = jax.scipy.linalg.cho_solve((factor, True), target)
    update = coeffs[0] * search[0]
    for iteration in range(1, ITERS):
        update = update + coeffs[iteration] * search[iteration]
    return (update, hessenberg)
```

```python
import functools

import jax
import jax.numpy as jnp
from jax import lax
from jax.experimental import pallas as pl
from jax.experimental.pallas import tpu as pltpu
from jax.sharding import PartitionSpec as P

ITERS = 3
LINES_DEV = 16
SUB = 8
MIB = 1 << 20
HIGHEST = lax.Precision.HIGHEST
F32 = jnp.float32
BF16 = jnp.bfloat16


def lanes_of(shape):
    return lax.broadcasted_iota(jnp.int32, shape, 1)


def fold_sublanes(parts):
    row = lax.broadcasted_iota(jnp.int32, parts[0].shape, 0)
    step = SUB // 2
    while step:
        mask = (row & step) == 0
        folded = []
        for a in range(step):
            low, high = parts[a], parts[a + step]
            if step == SUB // 2:
                kept = jnp.where(mask, low, high)
                folded.append(kept + pltpu.roll(jnp.where(mask, high, low), step, 0))
            else:
                low = low + pltpu.roll(low, SUB - step, 0)
                high = high + pltpu.roll(high, step, 0)
                folded.append(jnp.where(mask, low, high))
        parts = folded
        step //= 2
    return parts[0]


def spread_groups(packed, width):
    total = packed.shape[1]
    group = lanes_of(packed.shape) // width
    step = total // width // 2
    arrays = [packed]
    while step:
        clear = (group & step) == 0
        grown = []
        for item in arrays:
            moved = pltpu.roll(item, step * width, 1)
            grown.append(jnp.where(clear, item, moved))
            grown.append(jnp.where(clear, moved, item))
        arrays = grown
        step //= 2
    return arrays


def swap_groups(arrays, width):
    count = len(arrays)
    total = arrays[0].shape[1]
    group = lanes_of(arrays[0].shape) // width
    arrays = list(arrays)
    step = count // 2
    while step:
        clear = (group & step) == 0
        for a in range(count):
            if a & step == 0:
                low, high = arrays[a], arrays[a + step]
                arrays[a] = jnp.where(clear, low, pltpu.roll(high, step * width, 1))
                arrays[a + step] = jnp.where(clear, pltpu.roll(low, total - step * width, 1), high)
        step //= 2
    return arrays


def group_zero(arrays, width):
    group = lanes_of(arrays[0].shape) // width
    packed = arrays[0]
    for g in range(1, len(arrays)):
        packed = jnp.where(group == g, pltpu.roll(arrays[g], g * width, 1), packed)
    return packed


def rows_of(array):
    return [array[SUB * g : SUB * (g + 1)] for g in range(array.shape[0] // SUB)]


def packed_product(blocks, packed, width):
    spread = spread_groups(packed, width)
    parts = []
    for il in range(SUB):
        rows = rows_of(blocks(il).astype(F32))
        terms = [rows[g] * spread[g] for g in range(len(rows))]
        while len(terms) > 1:
            terms = [terms[t] + terms[t + 1] for t in range(0, len(terms), 2)]
        parts.append(terms[0])
    return fold_sublanes(parts)


def block_rows(reads, vectors):
    parts = []
    for i in range(SUB):
        total = None
        for read, vector in zip(reads, vectors):
            rows = rows_of(read(i).astype(F32))
            for row, entry in zip(rows, vector):
                term = row * entry
                total = term if total is None else total + term
        parts.append(total)
    return fold_sublanes(parts)


def swap_sublanes(arrays):
    row = lax.broadcasted_iota(jnp.int32, arrays[0].shape, 0)
    arrays = list(arrays)
    step = SUB // 2
    while step:
        clear = (row & step) == 0
        for a in range(SUB):
            if a & step == 0:
                low, high = arrays[a], arrays[a + step]
                arrays[a] = jnp.where(clear, low, pltpu.roll(high, step, 0))
                arrays[a + step] = jnp.where(clear, pltpu.roll(low, SUB - step, 0), high)
        step //= 2
    return arrays


def steps_kernel(width, fwd, bwd, fwd_steps, bwd_steps, last):
    size, _, elements = fwd.shape
    positions = elements // width
    pack = 2 * SUB
    split = size // pack

    @pl.loop(0, SUB * split)
    def _(n):
        il = n // split
        at = pl.multiple_of((n % split) * pack, pack)
        for blocks, steps in ((fwd, fwd_steps), (bwd, bwd_steps)):
            arrays = [
                -blocks[ih * SUB + il, pl.ds(at, pack), :].astype(F32) for ih in range(size // SUB)
            ]
            arrays = swap_groups(arrays, width)
            for q in range(positions):
                steps[q, il, pl.ds(at, pack), :] = arrays[q].astype(BF16)
            if steps is bwd_steps:
                last[il, pl.ds(at, pack), :] = arrays[-1].astype(BF16)


def step_layouts(fwd, bwd, width):
    size, _, elements = fwd.shape
    steps = jax.ShapeDtypeStruct((elements // width, SUB, size, elements), BF16)
    return pl.pallas_call(
        functools.partial(steps_kernel, width),
        out_shape=(steps, steps, jax.ShapeDtypeStruct((SUB, size, elements), BF16)),
        name="step_layouts",
        compiler_params=pltpu.CompilerParams(vmem_limit_bytes=10 * MIB),
        cost_estimate=pl.CostEstimate(flops=4000000, bytes_accessed=8 * MIB, transcendentals=0),
    )(fwd, bwd)


def chain_kernel(width, fwd, bwd, response, ends, tiles, chain):
    size, _, elements = fwd.shape
    positions = elements // width
    half = lanes_of((size, elements)) < size

    @pl.loop(0, size // SUB)
    def _(n):
        turned = []
        for il in range(SUB):
            both = jnp.concatenate(
                [fwd[n * SUB + il].astype(F32), bwd[n * SUB + il].astype(F32)], axis=0
            )
            turned.append(-both.T)
        for g in range(elements // SUB):
            rows = swap_sublanes([t[g * SUB : (g + 1) * SUB] for t in turned])
            for a in range(SUB):
                tiles[pl.ds((g * SUB + a) * size + n * SUB, SUB), :] = rows[a]

    def tile(e):
        return tiles[pl.ds(pl.multiple_of(e * size, size), size), :]

    def split(value):
        high = value.astype(BF16)
        return high, (value - high.astype(F32)).astype(BF16)

    zeros = jnp.zeros((size, 2 * elements), BF16)
    for line in range(width):
        first = tile(line)
        chain[pl.ds(line * size, size), :] = jnp.where(half, first, pltpu.roll(first, size, 1))

    @pl.loop(1, positions)
    def _(q):
        for line in range(width):
            e = q * width + line
            before = chain[pl.ds(pl.multiple_of((e - width) * size, size), size), :]
            high, low = split(before)
            right = jnp.where(half, high, low)
            out = jnp.dot(tile(e)[:, :size].astype(BF16), right, preferred_element_type=F32)
            chain[pl.ds(pl.multiple_of(e * size, size), size), :] = out + pltpu.roll(out, size, 1)

    last = positions - 1
    paired = width // 2
    for line in range(paired):
        e = last * width + line
        one = chain[pl.ds(e * size, size), :]
        two = chain[pl.ds((e + paired) * size, size), :]
        ends[line] = jnp.where(half, one, two)
    for line in range(width):
        e = last * width + line
        chain[pl.ds(e * size, size), :] = jnp.where(half, chain[pl.ds(e * size, size), :], tile(e))

    @pl.loop(0, last)
    def _(n):
        q = last - 1 - n
        for line in range(width):
            e = q * width + line
            after = chain[pl.ds(pl.multiple_of((e + width) * size, size), size), :]
            high, low = split(after)
            right = jnp.concatenate([zeros, jnp.concatenate([high, low], axis=1)], axis=0)
            out = jnp.dot(tile(e).astype(BF16), right, preferred_element_type=F32)
            own = chain[pl.ds(pl.multiple_of(e * size, size), size), :]
            chain[pl.ds(pl.multiple_of(e * size, size), size), :] = (
                jnp.where(half, own, 0.0) + out[:, :elements] + out[:, elements:]
            )

    for line in range(width):
        ends[paired + line] = chain[pl.ds(line * size, size), :]

    @pl.loop(0, size // SUB)
    def _(n):
        groups = []
        for g in range(elements // SUB):
            groups.append(
                swap_sublanes(
                    [chain[pl.ds((g * SUB + a) * size + n * SUB, SUB), :] for a in range(SUB)]
                )
            )
        for il in range(SUB):
            response[n * SUB + il] = jnp.concatenate([rows[il] for rows in groups], axis=0).T


def chain_products(fwd, bwd, width):
    size, _, elements = fwd.shape
    return pl.pallas_call(
        functools.partial(chain_kernel, width),
        out_shape=(
            jax.ShapeDtypeStruct((size, 2 * size, elements), F32),
            jax.ShapeDtypeStruct((width + width // 2, size, elements), F32),
        ),
        scratch_shapes=[
            pltpu.VMEM((elements * size, elements), F32),
            pltpu.VMEM((elements * size, elements), F32),
        ],
        name="chain_products",
        compiler_params=pltpu.CompilerParams(vmem_limit_bytes=20 * MIB),
        cost_estimate=pl.CostEstimate(flops=40000000, bytes_accessed=12 * MIB, transcendentals=0),
    )(fwd, bwd)


def maps_kernel(width, own, other, through_low, through_high, reach_high, back_low, back_high, pair):
    size = own.shape[1]
    elements = own.shape[2]
    is_odd = lax.axis_index("line") % 2 == 1
    half = lanes_of((size, elements)) < size
    paired = width // 2

    def through(line, which):
        both = which(line % paired)
        turned = pltpu.roll(both, size, 1)
        return (both, turned) if line < paired else (turned, both)

    def low(n):
        return jnp.where(is_odd, other[n], own[n])

    def high(n):
        return jnp.where(is_odd, own[n], other[n])

    def pack(tile, outs):
        groups = []
        for ih in range(size // SUB):
            for lh in range(width // SUB):
                groups.append(
                    swap_sublanes(
                        [tile(lh * SUB + a)[ih * SUB : (ih + 1) * SUB] for a in range(SUB)]
                    )
                )
        for il in range(SUB):
            turned = jnp.concatenate([rows[il] for rows in groups], axis=0).T
            for n, out in enumerate(outs):
                out[il] = turned[n * size : (n + 1) * size]

    def joined(line):
        left, right = through(line, low)
        both = jnp.where(half, left, right)
        top, bottom = high(paired + line), low(paired + line)
        step = jnp.dot(top[:, :size], both, precision=HIGHEST, preferred_element_type=F32)
        turned = pltpu.roll(bottom, size, 1)
        step = jnp.dot(turned[:, :size], step, precision=HIGHEST, preferred_element_type=F32)
        return jnp.where(half, pltpu.roll(top, size, 1), turned + step)

    first = [
        jnp.where(half, through(line, low)[0], through(line, high)[1]) for line in range(width)
    ]
    pack(lambda line: first[line], (through_low, through_high))
    second = [jnp.where(half, high(paired + line), low(paired + line)) for line in range(width)]
    pack(lambda line: second[line], (reach_high, back_low))
    third = [joined(line) for line in range(width)]
    pack(lambda line: third[line], (back_high, pair))


def maps(own, other, width):
    size, elements = own.shape[1:]
    shape = jax.ShapeDtypeStruct((SUB, size, elements), F32)
    return pl.pallas_call(
        functools.partial(maps_kernel, width),
        out_shape=(shape,) * 6,
        name="line_maps",
        compiler_params=pltpu.CompilerParams(vmem_limit_bytes=10 * MIB),
    )(own, other)


def line_sweeps(width, entries, inv, fwd_steps, bwd_steps, local, ends, source):
    elements = source.shape[1]
    positions = elements // width

    @pl.loop(0, source.shape[0] // SUB)
    def _(n):
        at = pl.multiple_of(n * SUB, SUB)
        source[pl.ds(at, SUB), :] = block_rows([lambda i: inv[at + i]], [entries])

    values = swap_groups(rows_of(source[...]), width)
    for q in range(1, positions):
        values[q] = values[q] + packed_product(lambda il: fwd_steps[q, il], values[q - 1], width)
    ends[:SUB] = values[-1]
    for q in reversed(range(positions - 1)):
        values[q] = values[q] + packed_product(lambda il: bwd_steps[q, il], values[q + 1], width)
    ends[SUB:] = values[0]
    for n, rows in enumerate(swap_groups(values, width)):
        local[SUB * n : SUB * (n + 1), :] = rows


def sweep_kernel(width, right_side, norm, inv, fwd_steps, bwd_steps, local, ends, vector, source):
    vector[...] = right_side[...] / norm[0:1, :]
    rounded = vector[...].astype(BF16).astype(F32)
    line_sweeps(width, rows_of(rounded), inv, fwd_steps, bwd_steps, local, ends, source)


def sweep_shapes(size, elements):
    return (
        jax.ShapeDtypeStruct((size, elements), F32),
        jax.ShapeDtypeStruct((2 * SUB, elements), F32),
        jax.ShapeDtypeStruct((size, elements), F32),
    )


def sweep(right_side, norm, inv, fwd_steps, bwd_steps, width):
    size, elements = right_side.shape
    return pl.pallas_call(
        functools.partial(sweep_kernel, width),
        out_shape=sweep_shapes(size, elements),
        scratch_shapes=[pltpu.VMEM((size, elements), F32)],
        name="line_sweep",
        compiler_params=pltpu.CompilerParams(vmem_limit_bytes=6 * MIB),
    )(right_side, norm, inv, fwd_steps, bwd_steps)


def low_high(own, other):
    is_odd = lax.axis_index("line") % 2 == 1
    mine, theirs = own[...], other[...]
    return is_odd, jnp.where(is_odd, theirs, mine), jnp.where(is_odd, mine, theirs)


def pair_kernel(width, own, other, through_high, reach_high, back_low, far_pair, ends, crossing):
    _, low, high = low_high(own, other)
    passed = high[:SUB] + packed_product(lambda il: through_high[il], low[:SUB], width)
    reached = high[SUB:] + packed_product(lambda il: reach_high[il], low[:SUB], width)
    ends[:SUB] = passed
    ends[SUB:] = low[SUB:] + packed_product(lambda il: back_low[il], reached, width)
    crossing[...] = packed_product(lambda il: far_pair[il], passed, width)


def pair_ends(own, other, through_high, reach_high, back_low, far_pair, width):
    return pl.pallas_call(
        functools.partial(pair_kernel, width),
        out_shape=(
            jax.ShapeDtypeStruct((2 * SUB, own.shape[1]), F32),
            jax.ShapeDtypeStruct((SUB, own.shape[1]), F32),
        ),
        name="line_pair",
        compiler_params=pltpu.CompilerParams(vmem_limit_bytes=4 * MIB),
    )(own, other, through_high, reach_high, back_low, far_pair)


def correct_kernel(
    width, own, other, crossing, far, local, through_low, reach_high, back_high, before_a, before_b,
    response, send_list, result, edges, sent,
):
    place = lax.axis_index("line")
    is_upper = place // 2 == 1
    is_odd, low, high = low_high(own, other)
    zero = jnp.zeros(low[:SUB].shape, F32)
    enter = jnp.where(is_upper, far[:SUB], zero)
    leave = jnp.where(is_upper, zero, far[SUB:] + crossing[...])
    middle = low[:SUB] + packed_product(lambda il: through_low[il], enter, width)
    meet = (
        high[SUB:]
        + packed_product(lambda il: back_high[il], leave, width)
        + packed_product(lambda il: reach_high[il], middle, width)
    )
    forward = jnp.where(is_odd, middle, enter)
    backward = jnp.where(is_odd, leave, meet)
    entries = spread_groups(forward, width) + spread_groups(backward, width)

    @pl.loop(0, local.shape[0] // SUB)
    def _(n):
        at = pl.multiple_of(n * SUB, SUB)
        result[pl.ds(at, SUB), :] = local[pl.ds(at, SUB), :] + block_rows(
            [lambda i: response[at + i]], [entries]
        )

    first = group_zero(rows_of(result[...]), width)
    back = packed_product(
        lambda il: jnp.where(is_odd, before_a[il].astype(F32), before_b[il].astype(F32)), first, width
    )
    edges[:SUB] = forward + jnp.where(place == 0, zero, back)
    edges[SUB:] = backward
    size, elements = result.shape
    rest = jnp.zeros((1, elements - send_list.shape[0] * send_list.shape[1]), jnp.int32)
    index = jnp.concatenate([send_list[0:1, :], send_list[1:2, :], rest], axis=1)
    index = jnp.broadcast_to(index, result.shape)
    sent[...] = jnp.take_along_axis(result[...], index, axis=1)[:, : sent.shape[1]]


def correct(own, other, crossing, far, local, through_low, reach_high, back_high, before_a, before_b, response, send_list, width):
    size, elements = local.shape
    return pl.pallas_call(
        functools.partial(correct_kernel, width),
        out_shape=(
            jax.ShapeDtypeStruct((size, elements), F32),
            jax.ShapeDtypeStruct((2 * SUB, elements), F32),
            jax.ShapeDtypeStruct((size, send_list.size), F32),
        ),
        name="line_correct",
        compiler_params=pltpu.CompilerParams(vmem_limit_bytes=10 * MIB),
    )(own, other, crossing, far, local, through_low, reach_high, back_high, before_a, before_b, response, send_list)


def near_kernel(width, rounded, vector, edges, diag, lower, upper, out):
    size, elements = vector.shape
    lane = lanes_of((SUB, elements))
    center = rows_of(vector[...])
    before = spread_groups(edges[:SUB], width)
    after = spread_groups(edges[SUB:], width)
    earlier = [
        jnp.where(lane < width, edge, pltpu.roll(rows, width, 1))
        for rows, edge in zip(center, before)
    ]
    later = [
        jnp.where(lane >= elements - width, edge, pltpu.roll(rows, elements - width, 1))
        for rows, edge in zip(center, after)
    ]
    if rounded:
        center, earlier, later = (
            [rows.astype(BF16).astype(F32) for rows in each] for each in (center, earlier, later)
        )

    @pl.loop(0, size // SUB)
    def _(n):
        at = pl.multiple_of(n * SUB, SUB)
        out[pl.ds(at, SUB), :] = block_rows(
            [lambda i: diag[at + i], lambda i: lower[at + i], lambda i: upper[at + i]],
            [center, earlier, later],
        )


def near(vector, edges, diag, lower, upper, width, rounded):
    size, elements = vector.shape
    return pl.pallas_call(
        functools.partial(near_kernel, width, rounded),
        out_shape=jax.ShapeDtypeStruct((size, elements), F32),
        name="near_faces",
        compiler_params=pltpu.CompilerParams(vmem_limit_bytes=6 * MIB),
        cost_estimate=pl.CostEstimate(
            flops=6 * size * size * elements, bytes_accessed=6 * size * size * elements, transcendentals=0
        ),
    )(vector, edges, diag, lower, upper)


def pick_faces(rounded, vector, got_a, got_b, face_nbr, picked):
    count, size, elements = picked.shape
    width = got_a.shape[1]
    halo = width // 2
    place, last = lax.axis_index("dom"), lax.axis_size("dom") - 1
    even = place % 2 == 0
    own = vector[...]
    halos = [got_a[...], got_b[...], jnp.zeros((size, elements - 2 * width), F32)]
    halos = jnp.concatenate(halos, axis=1)
    for f in range(count):
        slot = face_nbr[f : f + 1, :]
        left = jnp.logical_and(slot < elements + halo, place > 0)
        right = jnp.logical_and(slot >= elements + halo, slot < elements + width)
        right = jnp.logical_and(right, place < last)
        at_left = slot - elements + jnp.where(even, width, 0)
        at_right = slot - elements + jnp.where(even, 0, width)
        outside = jnp.where(left, at_left, jnp.where(right, at_right, 2 * width))
        at = jnp.broadcast_to(slot, (size, elements))
        outside = jnp.broadcast_to(jnp.clip(outside, 0, elements - 1), (size, elements))
        inner = jnp.take_along_axis(own, jnp.clip(at, 0, elements - 1), axis=1)
        outer = jnp.take_along_axis(halos, outside, axis=1)
        chosen = jnp.where(at < elements, inner, outer)
        if rounded:
            chosen = chosen.astype(BF16).astype(F32)
        picked[f] = chosen


def add_faces(partial, faces, picked, out):
    count, size, elements = picked.shape
    reads = [functools.partial(lambda f, at, i: faces[f, at + i], f) for f in range(count)]

    @pl.loop(0, size // SUB)
    def _(n):
        at = pl.multiple_of(n * SUB, SUB)
        vectors = [rows_of(picked[f]) for f in range(count)]
        out[pl.ds(at, SUB), :] = partial[pl.ds(at, SUB), :] + block_rows(
            [functools.partial(read, at) for read in reads], vectors
        )


def advance_kernel(
    width, rounded, vector, got_a, got_b, face_nbr, partial, faces, inv, fwd_steps, bwd_steps,
    local, ends, out, picked, source,
):
    pick_faces(rounded, vector, got_a, got_b, face_nbr, picked)
    add_faces(partial, faces, picked, out)
    line_sweeps(width, rows_of(out[...]), inv, fwd_steps, bwd_steps, local, ends, source)


def advance(vector, got_a, got_b, face_nbr, partial, faces, inv, fwd_steps, bwd_steps, width, rounded):
    size, elements = vector.shape
    return pl.pallas_call(
        functools.partial(advance_kernel, width, rounded),
        out_shape=sweep_shapes(size, elements),
        scratch_shapes=[
            pltpu.VMEM((faces.shape[0], size, elements), F32),
            pltpu.VMEM((size, elements), F32),
        ],
        name="faces_and_sweep",
        compiler_params=pltpu.CompilerParams(vmem_limit_bytes=10 * MIB),
    )(vector, got_a, got_b, face_nbr, partial, faces, inv, fwd_steps, bwd_steps)


def closing_kernel(rounded, vector, got_a, got_b, face_nbr, partial, faces, *rest):
    basis, (sums, last, picked) = rest[:-3], rest[-3:]
    pick_faces(rounded, vector, got_a, got_b, face_nbr, picked)
    add_faces(partial, faces, picked, last)
    vectors = [rows_of(each[...]) for each in basis] + [rows_of(last[...])]
    lines = []
    for i in range(len(vectors)):
        for j in range(i, len(vectors)):
            lines.append(sum(a * b for a, b in zip(vectors[i], vectors[j])))
    while len(lines) % SUB:
        lines.append(jnp.zeros_like(lines[0]))
    for n in range(0, len(lines), SUB):
        folded = fold_sublanes(lines[n : n + SUB])
        sums[n : n + SUB, :] = jnp.broadcast_to(jnp.sum(folded, axis=1, keepdims=True), folded.shape)


def closing(vector, got_a, got_b, face_nbr, partial, faces, basis, rounded):
    size, elements = vector.shape
    count = len(basis) + 1
    rows = count * (count + 1) // 2
    rows += -rows % SUB
    return pl.pallas_call(
        functools.partial(closing_kernel, rounded),
        out_shape=jax.ShapeDtypeStruct((rows, elements), F32),
        scratch_shapes=[
            pltpu.VMEM((size, elements), F32),
            pltpu.VMEM((faces.shape[0], size, elements), F32),
        ],
        name="faces_and_sums",
        compiler_params=pltpu.CompilerParams(vmem_limit_bytes=8 * MIB),
    )(vector, got_a, got_b, face_nbr, partial, faces, *basis)


def cholesky(entry, count):
    tri = {}
    for i in range(count):
        pivot = entry[i, i]
        for k in range(i):
            pivot = pivot - tri[k, i] * tri[k, i]
        tri[i, i] = jnp.sqrt(pivot)
        for j in range(i + 1, count):
            value = entry[i, j]
            for k in range(i):
                value = value - tri[k, i] * tri[k, j]
            tri[i, j] = value / tri[i, i]
    return tri


def finish_kernel(iters, norm, sums, *rest):
    search, (update, hessenberg) = rest[:iters], rest[iters:]
    count = iters + 1
    entry = {}
    n = 0
    for i in range(count):
        for j in range(i, count):
            entry[i, j] = sums[n : n + 1, :]
            n += 1
    tri = cholesky(entry, count)
    hess = {}
    for j in range(iters):
        for i in range(j + 2):
            value = tri[i, j + 1]
            for k in range(max(i - 1, 0), j):
                value = value - hess[i, k] * tri[k, j]
            hess[i, j] = value / tri[j, j]
    shape = (count, norm.shape[1])
    row, column = (lax.broadcasted_iota(jnp.int32, shape, axis) for axis in (0, 1))
    table = jnp.zeros(shape, F32)
    for (i, j), value in hess.items():
        table = jnp.where(jnp.logical_and(row == i, column == j), value, table)
    hessenberg[...] = table[:, :iters]
    normal = {}
    for i in range(iters):
        for j in range(i, iters):
            normal[i, j] = sum(hess[k, i] * hess[k, j] for k in range(i + 2))
    factor = cholesky(normal, iters)
    start = norm[0:1, :] * tri[0, 0]
    half = []
    for i in range(iters):
        value = start * hess[0, i]
        for k in range(i):
            value = value - factor[k, i] * half[k]
        half.append(value / factor[i, i])
    coeffs = [None] * iters
    for i in reversed(range(iters)):
        value = half[i]
        for k in range(i + 1, iters):
            value = value - factor[i, k] * coeffs[k]
        coeffs[i] = value / factor[i, i]
    weights = [None] * iters
    for i in reversed(range(iters)):
        value = coeffs[i]
        for k in range(i + 1, iters):
            value = value - tri[i, k] * weights[k]
        weights[i] = value / tri[i, i]
    update[...] = sum(weights[i] * search[i][...] for i in range(iters))


def finish(norm, sums, search):
    iters = len(search)
    size, elements = search[0].shape
    return pl.pallas_call(
        functools.partial(finish_kernel, iters),
        out_shape=(
            jax.ShapeDtypeStruct((size, elements), F32),
            jax.ShapeDtypeStruct((iters + 1, iters), F32),
        ),
        name="solve_and_update",
        compiler_params=pltpu.CompilerParams(vmem_limit_bytes=2 * MIB),
    )(norm, sums, *search)


def flip(count, bit):
    return [(i, i ^ bit) for i in range(count)]


def neighbour_pairs(count):
    pairs = []
    for i in range(count):
        j = i + 1 if i % 2 else i - 1
        pairs.append((i, j if 0 <= j < count else i))
    return pairs


def sum_all(value):
    axes = ("dom", "line")
    doms, lines = lax.axis_size("dom"), lax.axis_size("line")
    total = doms * lines
    bits = []
    bit = 1
    while bit < total:
        bits.append(bit)
        bit *= 2
    groups = [bits[:1]] + [bits[n : n + 2] for n in range(1, len(bits), 2)]
    for group in groups:
        masks = [0]
        for bit in group:
            masks = masks + [m | bit for m in masks]
        value = sum((lax.ppermute(value, axes, flip(total, m)) for m in masks[1:]), value)
    return value


def shards(
    right_side, diag_blocks, lower_blocks, upper_blocks, face_blocks, face_nbr, send_list,
    inv_blocks, fwd_blocks, bwd_blocks,
):
    width = LINES_DEV
    lines, doms = lax.axis_size("line"), lax.axis_size("dom")

    squares = jnp.broadcast_to(jnp.sum(right_side * right_side), (SUB, right_side.shape[1]))
    norm = jnp.sqrt(sum_all(squares))
    fwd_steps, bwd_steps, last_block = step_layouts(fwd_blocks, bwd_blocks, width)
    before_a = lax.ppermute(last_block, "line", flip(lines, 1))
    before_b = lax.ppermute(last_block, "line", neighbour_pairs(lines))
    response, ends = chain_products(fwd_blocks, bwd_blocks, width)
    other_ends = lax.ppermute(ends, "line", flip(lines, 1))
    through_low, through_high, reach_high, back_low, back_high, pair = maps(ends, other_ends, width)
    far_pair = lax.ppermute(pair, "line", flip(lines, 2))

    local, ends_own, first = sweep(right_side, norm, inv_blocks, fwd_steps, bwd_steps, width)
    basis = [first]
    search = []
    for iteration in range(ITERS):
        rounded = iteration == 0
        ends_other = lax.ppermute(ends_own, "line", flip(lines, 1))
        pair_own, crossing = pair_ends(
            ends_own, ends_other, through_high, reach_high, back_low, far_pair, width
        )
        pair_far = lax.ppermute(pair_own, "line", flip(lines, 2))
        direction, edges, sent = correct(
            ends_own, ends_other, crossing, pair_far, local, through_low, reach_high, back_high,
            before_a, before_b, response, send_list, width,
        )
        search.append(direction)
        got_a = lax.ppermute(sent, "dom", flip(doms, 1))
        got_b = lax.ppermute(sent, "dom", neighbour_pairs(doms))
        partial = near(direction, edges, diag_blocks, lower_blocks, upper_blocks, width, rounded)
        given = (direction, got_a, got_b, face_nbr, partial, face_blocks)
        if iteration + 1 < ITERS:
            local, ends_own, following = advance(
                *given, inv_blocks, fwd_steps, bwd_steps, width, rounded
            )
            basis.append(following)
    sums = sum_all(closing(*given, basis, rounded))
    update, hessenberg = finish(norm, sums, search)
    return (update, hessenberg)


def solution(mesh):
    in_specs = (
        P(None, ("dom", "line")),
        P(None, None, ("dom", "line")),
        P(None, None, ("dom", "line")),
        P(None, None, ("dom", "line")),
        P(None, None, None, ("dom", "line")),
        P(None, ("dom", "line")),
        P(None, ("dom", "line")),
        P(None, None, ("dom", "line")),
        P(None, None, ("dom", "line")),
        P(None, None, ("dom", "line")),
    )
    out_specs = (P(None, ("dom", "line")), P())
    return jax.shard_map(shards, mesh=mesh, in_specs=in_specs, out_specs=out_specs, check_vma=False)
```

```python
import functools

import jax
import jax.numpy as jnp
from jax import lax
from jax.experimental import pallas as pl
from jax.experimental.pallas import tpu as pltpu
from jax.sharding import PartitionSpec as P


ITERS = 3
LINES_DEV = 16
SUB = 8
MIB = 1 << 20
HIGHEST = lax.Precision.HIGHEST
F32 = jnp.float32
BF16 = jnp.bfloat16


def lanes_of(shape):
    return lax.broadcasted_iota(jnp.int32, shape, 1)


def fold_sublanes(parts):
    row = lax.broadcasted_iota(jnp.int32, parts[0].shape, 0)
    step = SUB // 2
    while step:
        mask = (row & step) == 0
        folded = []
        for a in range(step):
            low, high = parts[a], parts[a + step]
            if step == SUB // 2:
                kept = jnp.where(mask, low, high)
                folded.append(kept + pltpu.roll(jnp.where(mask, high, low), step, 0))
            else:
                low = low + pltpu.roll(low, SUB - step, 0)
                high = high + pltpu.roll(high, step, 0)
                folded.append(jnp.where(mask, low, high))
        parts = folded
        step //= 2
    return parts[0]


def choose(arrays, index):
    step = 1
    while len(arrays) > 1:
        clear = (index & step) == 0
        arrays = [jnp.where(clear, arrays[a], arrays[a + 1]) for a in range(0, len(arrays), 2)]
        step *= 2
    return arrays[0]


def spread_groups(packed, width):
    count = packed.shape[1] // width
    group = lanes_of(packed.shape) // width
    moved = [packed] + [pltpu.roll(packed, step * width, 1) for step in range(1, count)]
    return [choose([moved[(g - v) % count] for g in range(count)], group) for v in range(count)]


def swap_groups(arrays, width):
    count = len(arrays)
    group = lanes_of(arrays[0].shape) // width
    moved = [
        [array] + [pltpu.roll(array, step * width, 1) for step in range(1, count)] for array in arrays
    ]
    return [choose([moved[a][(a - q) % count] for a in range(count)], group) for q in range(count)]


def group_zero(arrays, width):
    group = lanes_of(arrays[0].shape) // width
    packed = arrays[0]
    for g in range(1, len(arrays)):
        packed = jnp.where(group == g, pltpu.roll(arrays[g], g * width, 1), packed)
    return packed


def rows_of(array):
    return [array[SUB * g : SUB * (g + 1)] for g in range(array.shape[0] // SUB)]


def packed_product(blocks, packed, width):
    spread = spread_groups(packed, width)
    parts = []
    for il in range(SUB):
        rows = rows_of(blocks(il).astype(F32))
        terms = [rows[g] * spread[g] for g in range(len(rows))]
        while len(terms) > 1:
            terms = [terms[t] + terms[t + 1] for t in range(0, len(terms), 2)]
        parts.append(terms[0])
    return fold_sublanes(parts)


def block_rows(reads, vectors):
    parts = []
    for i in range(SUB):
        total = None
        for read, vector in zip(reads, vectors):
            rows = rows_of(read(i).astype(F32))
            for row, entry in zip(rows, vector):
                term = row * entry
                total = term if total is None else total + term
        parts.append(total)
    return fold_sublanes(parts)


def swap_sublanes(arrays):
    row = lax.broadcasted_iota(jnp.int32, arrays[0].shape, 0)
    arrays = list(arrays)
    step = SUB // 2
    while step:
        clear = (row & step) == 0
        for a in range(SUB):
            if a & step == 0:
                low, high = arrays[a], arrays[a + step]
                arrays[a] = jnp.where(clear, low, pltpu.roll(high, step, 0))
                arrays[a + step] = jnp.where(clear, pltpu.roll(low, SUB - step, 0), high)
        step //= 2
    return arrays


def tiles_kernel(fwd, bwd, tiles):
    size, _, elements = fwd.shape

    @pl.loop(0, size // SUB)
    def _(n):
        turned = []
        for il in range(SUB):
            both = jnp.concatenate(
                [fwd[n * SUB + il].astype(F32), bwd[n * SUB + il].astype(F32)], axis=0
            )
            turned.append(-both.T)
        for g in range(elements // SUB):
            rows = swap_sublanes([t[g * SUB : (g + 1) * SUB] for t in turned])
            for a in range(SUB):
                tiles[pl.ds((g * SUB + a) * size + n * SUB, SUB), :] = rows[a]


def tile_layouts(fwd, bwd):
    size, _, elements = fwd.shape
    return pl.pallas_call(
        tiles_kernel,
        out_shape=jax.ShapeDtypeStruct((elements * size, 2 * size), F32),
        name="tile_layouts",
        compiler_params=pltpu.CompilerParams(vmem_limit_bytes=10 * MIB),
        cost_estimate=pl.CostEstimate(flops=4000000, bytes_accessed=10 * MIB, transcendentals=0),
    )(fwd, bwd)


def squares_kernel(vector, squares):
    total = sum(rows * rows for rows in rows_of(vector[...]))
    total = jnp.sum(jnp.sum(total, axis=1, keepdims=True), axis=0, keepdims=True)
    squares[...] = jnp.broadcast_to(total, squares.shape)


def sum_squares(vector):
    return pl.pallas_call(
        squares_kernel,
        out_shape=jax.ShapeDtypeStruct((SUB, vector.shape[1]), F32),
        name="sum_squares",
        compiler_params=pltpu.CompilerParams(vmem_limit_bytes=MIB),
    )(vector)


def chain_kernel(width, size, tiles, fwd_steps, bwd_steps, response, ends, chain):
    elements = tiles.shape[0] // size
    positions = elements // width
    half = lanes_of((size, elements)) < size

    def tile(e):
        return tiles[pl.ds(pl.multiple_of(e * size, size), size), :]

    def split(value):
        high = value.astype(BF16)
        return high, (value - high.astype(F32)).astype(BF16)

    zeros = jnp.zeros((size, 2 * elements), BF16)
    for line in range(width):
        first = tile(line)
        chain[pl.ds(line * size, size), :] = jnp.where(half, first, pltpu.roll(first, size, 1))

    def form_steps(q):
        groups = []
        for ih in range(size // SUB):
            for lh in range(width // SUB):
                start = (q * width + lh * SUB) * size + ih * SUB
                groups.append(
                    swap_sublanes([tiles[pl.ds(start + a * size, SUB), :] for a in range(SUB)])
                )
        for il in range(SUB):
            turned = jnp.concatenate([rows[il] for rows in groups], axis=0).T
            fwd_steps[q, il] = turned[:size].astype(BF16)
            bwd_steps[q, il] = turned[size:].astype(BF16)

    @pl.loop(1, positions)
    def _(q):
        form_steps(q)
        for line in range(width):
            e = q * width + line
            before = chain[pl.ds(pl.multiple_of((e - width) * size, size), size), :]
            high, low = split(before)
            right = jnp.where(half, high, low)
            out = jnp.dot(tile(e)[:, :size].astype(BF16), right, preferred_element_type=F32)
            chain[pl.ds(pl.multiple_of(e * size, size), size), :] = out + pltpu.roll(out, size, 1)

    form_steps(0)
    last = positions - 1
    paired = width // 2
    for line in range(paired):
        e = last * width + line
        one = chain[pl.ds(e * size, size), :]
        two = chain[pl.ds((e + paired) * size, size), :]
        ends[line] = jnp.where(half, one, two)
    for line in range(width):
        e = last * width + line
        chain[pl.ds(e * size, size), :] = jnp.where(half, chain[pl.ds(e * size, size), :], tile(e))

    @pl.loop(0, last)
    def _(n):
        q = last - 1 - n
        for line in range(width):
            e = q * width + line
            after = chain[pl.ds(pl.multiple_of((e + width) * size, size), size), :]
            high, low = split(after)
            right = jnp.concatenate([zeros, jnp.concatenate([high, low], axis=1)], axis=0)
            out = jnp.dot(tile(e).astype(BF16), right, preferred_element_type=F32)
            own = chain[pl.ds(pl.multiple_of(e * size, size), size), :]
            chain[pl.ds(pl.multiple_of(e * size, size), size), :] = (
                jnp.where(half, own, 0.0) + out[:, :elements] + out[:, elements:]
            )

    for line in range(width):
        ends[paired + line] = chain[pl.ds(line * size, size), :]
    ends[paired + width :] = bwd_steps[last].astype(F32)

    @pl.loop(0, size // SUB)
    def _(n):
        groups = []
        for g in range(elements // SUB):
            groups.append(
                swap_sublanes(
                    [chain[pl.ds((g * SUB + a) * size + n * SUB, SUB), :] for a in range(SUB)]
                )
            )
        for il in range(SUB):
            response[n * SUB + il] = jnp.concatenate([rows[il] for rows in groups], axis=0).T


def chain_products(tiles, width):
    elements = tiles.shape[1]
    size = tiles.shape[0] // elements
    steps = jax.ShapeDtypeStruct((elements // width, SUB, size, elements), BF16)
    return pl.pallas_call(
        functools.partial(chain_kernel, width, size),
        out_shape=(
            steps,
            steps,
            jax.ShapeDtypeStruct((size, 2 * size, elements), F32),
            jax.ShapeDtypeStruct((width + width // 2 + SUB, size, elements), F32),
        ),
        scratch_shapes=[pltpu.VMEM((elements * size, elements), F32)],
        name="chain_products",
        compiler_params=pltpu.CompilerParams(vmem_limit_bytes=16 * MIB),
        cost_estimate=pl.CostEstimate(flops=40000000, bytes_accessed=12 * MIB, transcendentals=0),
    )(tiles)


def maps_kernel(
    width, own, other, through_low, through_high, reach_high, back_low, back_high, before, message, pair
):
    size = own.shape[1]
    elements = own.shape[2]
    is_odd = lax.axis_index("line") % 2 == 1
    half = lanes_of((size, elements)) < size
    paired = width // 2

    def through(line, which):
        both = which(line % paired)
        turned = pltpu.roll(both, size, 1)
        return (both, turned) if line < paired else (turned, both)

    def low(n):
        return jnp.where(is_odd, other[n], own[n])

    def high(n):
        return jnp.where(is_odd, own[n], other[n])

    def pack(tile, outs):
        groups = []
        for ih in range(size // SUB):
            for lh in range(width // SUB):
                groups.append(
                    swap_sublanes(
                        [tile(lh * SUB + a)[ih * SUB : (ih + 1) * SUB] for a in range(SUB)]
                    )
                )
        for il in range(SUB):
            turned = jnp.concatenate([rows[il] for rows in groups], axis=0).T
            for n, out in enumerate(outs):
                out[il] = turned[n * size : (n + 1) * size]

    def joined(line):
        left, right = through(line, low)
        both = jnp.where(half, left, right)
        top, bottom = high(paired + line), low(paired + line)
        step = jnp.dot(top[:, :size], both, precision=HIGHEST, preferred_element_type=F32)
        turned = pltpu.roll(bottom, size, 1)
        step = jnp.dot(turned[:, :size], step, precision=HIGHEST, preferred_element_type=F32)
        return jnp.where(half, pltpu.roll(top, size, 1), turned + step)

    first = [
        jnp.where(half, through(line, low)[0], through(line, high)[1]) for line in range(width)
    ]
    pack(lambda line: first[line], (through_low, through_high))
    second = [jnp.where(half, high(paired + line), low(paired + line)) for line in range(width)]
    pack(lambda line: second[line], (reach_high, back_low))
    third = [joined(line) for line in range(width)]
    pack(lambda line: third[line], (back_high, pair))
    for il in range(SUB):
        top = pair[il].astype(BF16)
        message[il] = top
        message[SUB + il] = (pair[il] - top.astype(F32)).astype(BF16)
        before[il] = other[paired + width + il]
        message[2 * SUB + il] = other[paired + width + il].astype(BF16)


def maps(own, other, width):
    size, elements = own.shape[1:]
    shape = jax.ShapeDtypeStruct((SUB, size, elements), F32)
    return pl.pallas_call(
        functools.partial(maps_kernel, width),
        out_shape=(shape,) * 6 + (jax.ShapeDtypeStruct((3 * SUB, size, elements), BF16),),
        scratch_shapes=[pltpu.VMEM((SUB, size, elements), F32)],
        name="line_maps",
        compiler_params=pltpu.CompilerParams(vmem_limit_bytes=10 * MIB),
    )(own, other)


def line_sweeps(width, entries, inv, fwd_steps, bwd_steps, local, ends, source):
    elements = source.shape[1]
    positions = elements // width

    @pl.loop(0, source.shape[0] // SUB)
    def _(n):
        at = pl.multiple_of(n * SUB, SUB)
        source[pl.ds(at, SUB), :] = block_rows([lambda i: inv[at + i]], [entries])

    values = swap_groups(rows_of(source[...]), width)
    for q in range(1, positions):
        values[q] = values[q] + packed_product(lambda il: fwd_steps[q, il], values[q - 1], width)
    ends[:SUB] = values[-1]
    for q in reversed(range(positions - 1)):
        values[q] = values[q] + packed_product(lambda il: bwd_steps[q, il], values[q + 1], width)
    ends[SUB:] = values[0]
    for n, rows in enumerate(swap_groups(values, width)):
        local[SUB * n : SUB * (n + 1), :] = rows


def sweep_kernel(width, right_side, norm, inv, fwd_steps, bwd_steps, local, ends, vector, source):
    vector[...] = right_side[...] / norm[0:1, :]
    rounded = vector[...].astype(BF16).astype(F32)
    line_sweeps(width, rows_of(rounded), inv, fwd_steps, bwd_steps, local, ends, source)


def sweep_shapes(size, elements):
    return (
        jax.ShapeDtypeStruct((size, elements), F32),
        jax.ShapeDtypeStruct((2 * SUB, elements), F32),
        jax.ShapeDtypeStruct((size, elements), F32),
    )


def sweep(right_side, norm, inv, fwd_steps, bwd_steps, width):
    size, elements = right_side.shape
    return pl.pallas_call(
        functools.partial(sweep_kernel, width),
        out_shape=sweep_shapes(size, elements),
        scratch_shapes=[pltpu.VMEM((size, elements), F32)],
        name="line_sweep",
        compiler_params=pltpu.CompilerParams(vmem_limit_bytes=6 * MIB),
    )(right_side, norm, inv, fwd_steps, bwd_steps)


def low_high(own, other):
    is_odd = lax.axis_index("line") % 2 == 1
    mine, theirs = own[...], other[...]
    return is_odd, jnp.where(is_odd, theirs, mine), jnp.where(is_odd, mine, theirs)


def pair_kernel(width, own, other, through_high, reach_high, back_low, ends):
    _, low, high = low_high(own, other)
    passed = high[:SUB] + packed_product(lambda il: through_high[il], low[:SUB], width)
    reached = high[SUB:] + packed_product(lambda il: reach_high[il], low[:SUB], width)
    ends[:SUB] = passed
    ends[SUB:] = low[SUB:] + packed_product(lambda il: back_low[il], reached, width)


def pair_ends(own, other, through_high, reach_high, back_low, width):
    return pl.pallas_call(
        functools.partial(pair_kernel, width),
        out_shape=jax.ShapeDtypeStruct((2 * SUB, own.shape[1]), F32),
        name="line_pair",
        compiler_params=pltpu.CompilerParams(vmem_limit_bytes=4 * MIB),
    )(own, other, through_high, reach_high, back_low)


def correct_kernel(
    width, own, other, pair, far, local, through_low, reach_high, back_high, before, far_maps,
    response, send_list, result, edges, sent,
):
    place = lax.axis_index("line")
    is_upper = place // 2 == 1
    is_odd, low, high = low_high(own, other)
    zero = jnp.zeros(low[:SUB].shape, F32)
    enter = jnp.where(is_upper, far[:SUB], zero)
    crossing = packed_product(
        lambda il: far_maps[il].astype(F32) + far_maps[SUB + il].astype(F32), pair[:SUB], width
    )
    leave = jnp.where(is_upper, zero, far[SUB:] + crossing)
    middle = low[:SUB] + packed_product(lambda il: through_low[il], enter, width)
    meet = (
        high[SUB:]
        + packed_product(lambda il: back_high[il], leave, width)
        + packed_product(lambda il: reach_high[il], middle, width)
    )
    forward = jnp.where(is_odd, middle, enter)
    backward = jnp.where(is_odd, leave, meet)
    entries = spread_groups(forward, width) + spread_groups(backward, width)

    @pl.loop(0, local.shape[0] // SUB)
    def _(n):
        at = pl.multiple_of(n * SUB, SUB)
        result[pl.ds(at, SUB), :] = local[pl.ds(at, SUB), :] + block_rows(
            [lambda i: response[at + i]], [entries]
        )

    first = group_zero(rows_of(result[...]), width)
    back = packed_product(
        lambda il: jnp.where(is_odd, before[il], far_maps[2 * SUB + il].astype(F32)), first, width
    )
    edges[:SUB] = forward + jnp.where(place == 0, zero, back)
    edges[SUB:] = backward
    _, elements = result.shape
    rest = jnp.zeros((1, elements - send_list.shape[0] * send_list.shape[1]), jnp.int32)
    index = jnp.concatenate([send_list[0:1, :], send_list[1:2, :], rest], axis=1)
    index = jnp.broadcast_to(index, result.shape)
    sent[...] = jnp.take_along_axis(result[...], index, axis=1)[:, : sent.shape[1]]


def correct(own, other, pair, far, local, through_low, reach_high, back_high, before, far_maps, response, send_list, width):
    size, elements = local.shape
    return pl.pallas_call(
        functools.partial(correct_kernel, width),
        out_shape=(
            jax.ShapeDtypeStruct((size, elements), F32),
            jax.ShapeDtypeStruct((2 * SUB, elements), F32),
            jax.ShapeDtypeStruct((size, send_list.size), F32),
        ),
        name="line_correct",
        compiler_params=pltpu.CompilerParams(vmem_limit_bytes=10 * MIB),
    )(own, other, pair, far, local, through_low, reach_high, back_high, before, far_maps, response, send_list)


def near_kernel(width, rounded, vector, edges, diag, lower, upper, out):
    size, elements = vector.shape
    lane = lanes_of((SUB, elements))
    center = rows_of(vector[...])
    before = spread_groups(edges[:SUB], width)
    after = spread_groups(edges[SUB:], width)
    earlier = [
        jnp.where(lane < width, edge, pltpu.roll(rows, width, 1))
        for rows, edge in zip(center, before)
    ]
    later = [
        jnp.where(lane >= elements - width, edge, pltpu.roll(rows, elements - width, 1))
        for rows, edge in zip(center, after)
    ]
    if rounded:
        center, earlier, later = (
            [rows.astype(BF16).astype(F32) for rows in each] for each in (center, earlier, later)
        )

    @pl.loop(0, size // SUB)
    def _(n):
        at = pl.multiple_of(n * SUB, SUB)
        out[pl.ds(at, SUB), :] = block_rows(
            [lambda i: diag[at + i], lambda i: lower[at + i], lambda i: upper[at + i]],
            [center, earlier, later],
        )


def near(vector, edges, diag, lower, upper, width, rounded):
    size, elements = vector.shape
    return pl.pallas_call(
        functools.partial(near_kernel, width, rounded),
        out_shape=jax.ShapeDtypeStruct((size, elements), F32),
        name="near_faces",
        compiler_params=pltpu.CompilerParams(vmem_limit_bytes=6 * MIB),
        cost_estimate=pl.CostEstimate(
            flops=6 * size * size * elements, bytes_accessed=6 * size * size * elements, transcendentals=0
        ),
    )(vector, edges, diag, lower, upper)


def pick_faces(rounded, vector, got_a, got_b, face_nbr, picked):
    count, size, elements = picked.shape
    width = got_a.shape[1]
    halo = width // 2
    place, last = lax.axis_index("dom"), lax.axis_size("dom") - 1
    even = place % 2 == 0
    own = vector[...]
    halos = [got_a[...], got_b[...], jnp.zeros((size, elements - 2 * width), F32)]
    halos = jnp.concatenate(halos, axis=1)
    for f in range(count):
        slot = face_nbr[f : f + 1, :]
        left = jnp.logical_and(slot < elements + halo, place > 0)
        right = jnp.logical_and(slot >= elements + halo, slot < elements + width)
        right = jnp.logical_and(right, place < last)
        at_left = slot - elements + jnp.where(even, width, 0)
        at_right = slot - elements + jnp.where(even, 0, width)
        outside = jnp.where(left, at_left, jnp.where(right, at_right, 2 * width))
        at = jnp.broadcast_to(slot, (size, elements))
        outside = jnp.broadcast_to(jnp.clip(outside, 0, elements - 1), (size, elements))
        inner = jnp.take_along_axis(own, jnp.clip(at, 0, elements - 1), axis=1)
        outer = jnp.take_along_axis(halos, outside, axis=1)
        chosen = jnp.where(at < elements, inner, outer)
        if rounded:
            chosen = chosen.astype(BF16).astype(F32)
        picked[f] = chosen


def add_faces(partial, faces, picked, out):
    count, size, _ = picked.shape
    reads = [functools.partial(lambda f, at, i: faces[f, at + i], f) for f in range(count)]

    @pl.loop(0, size // SUB)
    def _(n):
        at = pl.multiple_of(n * SUB, SUB)
        vectors = [rows_of(picked[f]) for f in range(count)]
        out[pl.ds(at, SUB), :] = partial[pl.ds(at, SUB), :] + block_rows(
            [functools.partial(read, at) for read in reads], vectors
        )


def advance_kernel(
    width, rounded, vector, got_a, got_b, face_nbr, partial, faces, inv, fwd_steps, bwd_steps,
    local, ends, out, picked, source,
):
    pick_faces(rounded, vector, got_a, got_b, face_nbr, picked)
    add_faces(partial, faces, picked, out)
    line_sweeps(width, rows_of(out[...]), inv, fwd_steps, bwd_steps, local, ends, source)


def advance(vector, got_a, got_b, face_nbr, partial, faces, inv, fwd_steps, bwd_steps, width, rounded):
    size, elements = vector.shape
    return pl.pallas_call(
        functools.partial(advance_kernel, width, rounded),
        out_shape=sweep_shapes(size, elements),
        scratch_shapes=[
            pltpu.VMEM((faces.shape[0], size, elements), F32),
            pltpu.VMEM((size, elements), F32),
        ],
        name="faces_and_sweep",
        compiler_params=pltpu.CompilerParams(vmem_limit_bytes=10 * MIB),
    )(vector, got_a, got_b, face_nbr, partial, faces, inv, fwd_steps, bwd_steps)


def closing_kernel(rounded, vector, got_a, got_b, face_nbr, partial, faces, *rest):
    basis, (sums, last, picked) = rest[:-3], rest[-3:]
    pick_faces(rounded, vector, got_a, got_b, face_nbr, picked)
    add_faces(partial, faces, picked, last)
    vectors = [rows_of(each[...]) for each in basis] + [rows_of(last[...])]
    lines = []
    for i in range(len(vectors)):
        for j in range(i, len(vectors)):
            lines.append(sum(a * b for a, b in zip(vectors[i], vectors[j])))
    while len(lines) % SUB:
        lines.append(jnp.zeros_like(lines[0]))
    for n in range(0, len(lines), SUB):
        folded = fold_sublanes(lines[n : n + SUB])
        sums[n : n + SUB, :] = jnp.broadcast_to(jnp.sum(folded, axis=1, keepdims=True), folded.shape)


def closing(vector, got_a, got_b, face_nbr, partial, faces, basis, rounded):
    size, elements = vector.shape
    count = len(basis) + 1
    rows = count * (count + 1) // 2
    rows += -rows % SUB
    return pl.pallas_call(
        functools.partial(closing_kernel, rounded),
        out_shape=jax.ShapeDtypeStruct((rows, elements), F32),
        scratch_shapes=[
            pltpu.VMEM((size, elements), F32),
            pltpu.VMEM((faces.shape[0], size, elements), F32),
        ],
        name="faces_and_sums",
        compiler_params=pltpu.CompilerParams(vmem_limit_bytes=8 * MIB),
    )(vector, got_a, got_b, face_nbr, partial, faces, *basis)


def cholesky(entry, count):
    tri = {}
    for i in range(count):
        pivot = entry[i, i]
        for k in range(i):
            pivot = pivot - tri[k, i] * tri[k, i]
        tri[i, i] = jnp.sqrt(pivot)
        for j in range(i + 1, count):
            value = entry[i, j]
            for k in range(i):
                value = value - tri[k, i] * tri[k, j]
            tri[i, j] = value / tri[i, i]
    return tri


def finish_kernel(iters, norm, sums, *rest):
    search, (update, hessenberg) = rest[:iters], rest[iters:]
    count = iters + 1
    entry = {}
    n = 0
    for i in range(count):
        for j in range(i, count):
            entry[i, j] = sums[n : n + 1, :]
            n += 1
    tri = cholesky(entry, count)
    hess = {}
    for j in range(iters):
        for i in range(j + 2):
            value = tri[i, j + 1]
            for k in range(max(i - 1, 0), j):
                value = value - hess[i, k] * tri[k, j]
            hess[i, j] = value / tri[j, j]
    shape = (count, norm.shape[1])
    row, column = (lax.broadcasted_iota(jnp.int32, shape, axis) for axis in (0, 1))
    table = jnp.zeros(shape, F32)
    for (i, j), value in hess.items():
        table = jnp.where(jnp.logical_and(row == i, column == j), value, table)
    hessenberg[...] = table[:, :iters]
    normal = {}
    for i in range(iters):
        for j in range(i, iters):
            normal[i, j] = sum(hess[k, i] * hess[k, j] for k in range(i + 2))
    factor = cholesky(normal, iters)
    start = norm[0:1, :] * tri[0, 0]
    half = []
    for i in range(iters):
        value = start * hess[0, i]
        for k in range(i):
            value = value - factor[k, i] * half[k]
        half.append(value / factor[i, i])
    coeffs = [None] * iters
    for i in reversed(range(iters)):
        value = half[i]
        for k in range(i + 1, iters):
            value = value - factor[i, k] * coeffs[k]
        coeffs[i] = value / factor[i, i]
    weights = [None] * iters
    for i in reversed(range(iters)):
        value = coeffs[i]
        for k in range(i + 1, iters):
            value = value - tri[i, k] * weights[k]
        weights[i] = value / tri[i, i]
    update[...] = sum(weights[i] * search[i][...] for i in range(iters))


def finish(norm, sums, search):
    iters = len(search)
    size, elements = search[0].shape
    return pl.pallas_call(
        functools.partial(finish_kernel, iters),
        out_shape=(
            jax.ShapeDtypeStruct((size, elements), F32),
            jax.ShapeDtypeStruct((iters + 1, iters), F32),
        ),
        name="solve_and_update",
        compiler_params=pltpu.CompilerParams(vmem_limit_bytes=2 * MIB),
    )(norm, sums, *search)


def flip(count, bit):
    return [(i, i ^ bit) for i in range(count)]


def neighbour_pairs(count):
    pairs = []
    for i in range(count):
        j = i + 1 if i % 2 else i - 1
        pairs.append((i, j if 0 <= j < count else i))
    return pairs


def sum_over(value, groups):
    axes = ("dom", "line")
    total = lax.axis_size("dom") * lax.axis_size("line")
    for group in groups:
        masks = [0]
        for bit in group:
            masks = masks + [m | bit for m in masks]
        value = sum((lax.ppermute(value, axes, flip(total, m)) for m in masks[1:]), value)
    return value


def index_bits(limit):
    return [1 << n for n in range((limit - 1).bit_length())]


def steps(
    right_side, diag_blocks, lower_blocks, upper_blocks, face_blocks, face_nbr, send_list,
    inv_blocks, fwd_blocks, bwd_blocks,
):
    width = LINES_DEV
    lines, doms = lax.axis_size("line"), lax.axis_size("dom")

    bits = index_bits(doms * lines)
    start, tiles = lax.optimization_barrier((right_side, tile_layouts(fwd_blocks, bwd_blocks)))
    squares = sum_over(sum_squares(start), [bits[1:3]])
    squares = sum_over(squares, [bits[n : n + 2] for n in range(3, len(bits), 2)])
    fwd_steps, bwd_steps, response, ends = chain_products(tiles, width)
    other_ends = lax.ppermute(ends, "line", flip(lines, 1))
    norm = jnp.sqrt(sum_over(squares, [bits[:1]]))
    through_low, through_high, reach_high, back_low, back_high, before, message = maps(
        ends, other_ends, width
    )
    far_maps = lax.ppermute(message, "line", flip(lines, 2))

    local, ends_own, first = sweep(right_side, norm, inv_blocks, fwd_steps, bwd_steps, width)
    basis = [first]
    search = []
    for iteration in range(ITERS):
        rounded = iteration == 0
        ends_other = lax.ppermute(ends_own, "line", flip(lines, 1))
        pair_own = pair_ends(ends_own, ends_other, through_high, reach_high, back_low, width)
        pair_far = lax.ppermute(pair_own, "line", flip(lines, 2))
        direction, edges, sent = correct(
            ends_own, ends_other, pair_own, pair_far, local, through_low, reach_high, back_high,
            before, far_maps, response, send_list, width,
        )
        search.append(direction)
        got_a = lax.ppermute(sent, "dom", flip(doms, 1))
        got_b = lax.ppermute(sent, "dom", neighbour_pairs(doms))
        partial = near(direction, edges, diag_blocks, lower_blocks, upper_blocks, width, rounded)
        given = (direction, got_a, got_b, face_nbr, partial, face_blocks)
        if iteration + 1 < ITERS:
            local, ends_own, following = advance(
                *given, inv_blocks, fwd_steps, bwd_steps, width, rounded
            )
            basis.append(following)
    groups = [bits[:1]] + [bits[n : n + 2] for n in range(1, len(bits), 2)]
    sums = sum_over(closing(*given, basis, rounded), groups)
    update, hessenberg = finish(norm, sums, search)
    return (update, hessenberg)


def solution(mesh):
    in_specs = (
        P(None, ("dom", "line")),
        P(None, None, ("dom", "line")),
        P(None, None, ("dom", "line")),
        P(None, None, ("dom", "line")),
        P(None, None, None, ("dom", "line")),
        P(None, ("dom", "line")),
        P(None, ("dom", "line")),
        P(None, None, ("dom", "line")),
        P(None, None, ("dom", "line")),
        P(None, None, ("dom", "line")),
    )
    out_specs = (P(None, ("dom", "line")), P())
    return jax.shard_map(steps, mesh=mesh, in_specs=in_specs, out_specs=out_specs, check_vma=False)
```

```python
import functools

import jax
import jax.numpy as jnp
from jax import lax
from jax.experimental import pallas as pl
from jax.experimental.pallas import tpu as pltpu
from jax.sharding import PartitionSpec as P


ITERS = 3
LINES_DEV = 16
SUB = 8
MIB = 1 << 20
INDEPENDENT = 0.01
HIGHEST = lax.Precision.HIGHEST
F32 = jnp.float32
BF16 = jnp.bfloat16


def lanes_of(shape):
    return lax.broadcasted_iota(jnp.int32, shape, 1)


def fold_sublanes(parts):
    row = lax.broadcasted_iota(jnp.int32, parts[0].shape, 0)
    step = SUB // 2
    while step:
        mask = (row & step) == 0
        folded = []
        for a in range(step):
            low, high = parts[a], parts[a + step]
            if step == SUB // 2:
                kept = jnp.where(mask, low, high)
                folded.append(kept + pltpu.roll(jnp.where(mask, high, low), step, 0))
            else:
                low = low + pltpu.roll(low, SUB - step, 0)
                high = high + pltpu.roll(high, step, 0)
                folded.append(jnp.where(mask, low, high))
        parts = folded
        step //= 2
    return parts[0]


def choose(arrays, index):
    step = 1
    while len(arrays) > 1:
        clear = (index & step) == 0
        arrays = [jnp.where(clear, arrays[a], arrays[a + 1]) for a in range(0, len(arrays), 2)]
        step *= 2
    return arrays[0]


def spread_groups(packed, width):
    count = packed.shape[1] // width
    group = lanes_of(packed.shape) // width
    moved = [packed] + [pltpu.roll(packed, step * width, 1) for step in range(1, count)]
    return [choose([moved[(g - v) % count] for g in range(count)], group) for v in range(count)]


def swap_groups(arrays, width):
    count = len(arrays)
    group = lanes_of(arrays[0].shape) // width
    moved = [
        [array] + [pltpu.roll(array, step * width, 1) for step in range(1, count)] for array in arrays
    ]
    return [choose([moved[a][(a - q) % count] for a in range(count)], group) for q in range(count)]


def group_zero(arrays, width):
    group = lanes_of(arrays[0].shape) // width
    packed = arrays[0]
    for g in range(1, len(arrays)):
        packed = jnp.where(group == g, pltpu.roll(arrays[g], g * width, 1), packed)
    return packed


def rows_of(array):
    return [array[SUB * g : SUB * (g + 1)] for g in range(array.shape[0] // SUB)]


def packed_product(blocks, packed, width):
    spread = spread_groups(packed, width)
    parts = []
    for il in range(SUB):
        rows = rows_of(blocks(il).astype(F32))
        terms = [rows[g] * spread[g] for g in range(len(rows))]
        while len(terms) > 1:
            terms = [terms[t] + terms[t + 1] for t in range(0, len(terms), 2)]
        parts.append(terms[0])
    return fold_sublanes(parts)


def block_rows(reads, vectors):
    parts = []
    for i in range(SUB):
        total = None
        for read, vector in zip(reads, vectors):
            rows = rows_of(read(i).astype(F32))
            for row, entry in zip(rows, vector):
                term = row * entry
                total = term if total is None else total + term
        parts.append(total)
    return fold_sublanes(parts)


def swap_sublanes(arrays):
    row = lax.broadcasted_iota(jnp.int32, arrays[0].shape, 0)
    arrays = list(arrays)
    step = SUB // 2
    while step:
        clear = (row & step) == 0
        for a in range(SUB):
            if a & step == 0:
                low, high = arrays[a], arrays[a + step]
                arrays[a] = jnp.where(clear, low, pltpu.roll(high, step, 0))
                arrays[a + step] = jnp.where(clear, pltpu.roll(low, SUB - step, 0), high)
        step //= 2
    return arrays


def tiles_kernel(fwd, bwd, tiles):
    size, _, elements = fwd.shape

    @pl.loop(0, size // SUB)
    def _(n):
        turned = []
        for il in range(SUB):
            both = jnp.concatenate(
                [fwd[n * SUB + il].astype(F32), bwd[n * SUB + il].astype(F32)], axis=0
            )
            turned.append(-both.T)
        for g in range(elements // SUB):
            rows = swap_sublanes([t[g * SUB : (g + 1) * SUB] for t in turned])
            for a in range(SUB):
                tiles[pl.ds((g * SUB + a) * size + n * SUB, SUB), :] = rows[a]


def tile_layouts(fwd, bwd):
    size, _, elements = fwd.shape
    return pl.pallas_call(
        tiles_kernel,
        out_shape=jax.ShapeDtypeStruct((elements * size, 2 * size), F32),
        name="tile_layouts",
        compiler_params=pltpu.CompilerParams(vmem_limit_bytes=10 * MIB),
        cost_estimate=pl.CostEstimate(flops=4000000, bytes_accessed=10 * MIB, transcendentals=0),
    )(fwd, bwd)


def squares_kernel(vector, squares):
    total = sum(rows * rows for rows in rows_of(vector[...]))
    total = jnp.sum(jnp.sum(total, axis=1, keepdims=True), axis=0, keepdims=True)
    squares[...] = jnp.broadcast_to(total, squares.shape)


def sum_squares(vector):
    return pl.pallas_call(
        squares_kernel,
        out_shape=jax.ShapeDtypeStruct((SUB, vector.shape[1]), F32),
        name="sum_squares",
        compiler_params=pltpu.CompilerParams(vmem_limit_bytes=MIB),
        cost_estimate=pl.CostEstimate(flops=10**10, bytes_accessed=64 * MIB, transcendentals=0),
    )(vector)


def chain_kernel(width, size, tiles, fwd_steps, bwd_steps, response, ends, chain):
    elements = tiles.shape[0] // size
    positions = elements // width
    half = lanes_of((size, elements)) < size

    def tile(e):
        return tiles[pl.ds(pl.multiple_of(e * size, size), size), :]

    def split(value):
        high = value.astype(BF16)
        return high, (value - high.astype(F32)).astype(BF16)

    zeros = jnp.zeros((size, 2 * elements), BF16)
    for line in range(width):
        first = tile(line)
        chain[pl.ds(line * size, size), :] = jnp.where(half, first, pltpu.roll(first, size, 1))

    def form_steps(q):
        groups = []
        for ih in range(size // SUB):
            for lh in range(width // SUB):
                start = (q * width + lh * SUB) * size + ih * SUB
                groups.append(
                    swap_sublanes([tiles[pl.ds(start + a * size, SUB), :] for a in range(SUB)])
                )
        for il in range(SUB):
            turned = jnp.concatenate([rows[il] for rows in groups], axis=0).T
            fwd_steps[q, il] = turned[:size].astype(BF16)
            bwd_steps[q, il] = turned[size:].astype(BF16)

    @pl.loop(1, positions)
    def _(q):
        form_steps(q)
        for line in range(width):
            e = q * width + line
            before = chain[pl.ds(pl.multiple_of((e - width) * size, size), size), :]
            high, low = split(before)
            right = jnp.where(half, high, low)
            out = jnp.dot(tile(e)[:, :size].astype(BF16), right, preferred_element_type=F32)
            chain[pl.ds(pl.multiple_of(e * size, size), size), :] = out + pltpu.roll(out, size, 1)

    form_steps(0)
    last = positions - 1
    paired = width // 2
    for line in range(paired):
        e = last * width + line
        one = chain[pl.ds(e * size, size), :]
        two = chain[pl.ds((e + paired) * size, size), :]
        ends[line] = jnp.where(half, one, two)
    for line in range(width):
        e = last * width + line
        chain[pl.ds(e * size, size), :] = jnp.where(half, chain[pl.ds(e * size, size), :], tile(e))

    @pl.loop(0, last)
    def _(n):
        q = last - 1 - n
        for line in range(width):
            e = q * width + line
            after = chain[pl.ds(pl.multiple_of((e + width) * size, size), size), :]
            high, low = split(after)
            right = jnp.concatenate([zeros, jnp.concatenate([high, low], axis=1)], axis=0)
            out = jnp.dot(tile(e).astype(BF16), right, preferred_element_type=F32)
            own = chain[pl.ds(pl.multiple_of(e * size, size), size), :]
            chain[pl.ds(pl.multiple_of(e * size, size), size), :] = (
                jnp.where(half, own, 0.0) + out[:, :elements] + out[:, elements:]
            )

    for line in range(width):
        ends[paired + line] = chain[pl.ds(line * size, size), :]
    ends[paired + width :] = bwd_steps[last].astype(F32)

    @pl.loop(0, size // SUB)
    def _(n):
        groups = []
        for g in range(elements // SUB):
            groups.append(
                swap_sublanes(
                    [chain[pl.ds((g * SUB + a) * size + n * SUB, SUB), :] for a in range(SUB)]
                )
            )
        for il in range(SUB):
            response[n * SUB + il] = jnp.concatenate([rows[il] for rows in groups], axis=0).T


def chain_products(tiles, width):
    elements = tiles.shape[1]
    size = tiles.shape[0] // elements
    steps = jax.ShapeDtypeStruct((elements // width, SUB, size, elements), BF16)
    return pl.pallas_call(
        functools.partial(chain_kernel, width, size),
        out_shape=(
            steps,
            steps,
            jax.ShapeDtypeStruct((size, 2 * size, elements), F32),
            jax.ShapeDtypeStruct((width + width // 2 + SUB, size, elements), F32),
        ),
        scratch_shapes=[pltpu.VMEM((elements * size, elements), F32)],
        name="chain_products",
        compiler_params=pltpu.CompilerParams(vmem_limit_bytes=16 * MIB),
        cost_estimate=pl.CostEstimate(flops=40000000, bytes_accessed=12 * MIB, transcendentals=0),
    )(tiles)


def maps_kernel(
    width, own, other, through_low, through_high, reach_high, back_low, back_high, before, message, pair
):
    size = own.shape[1]
    elements = own.shape[2]
    is_odd = lax.axis_index("line") % 2 == 1
    half = lanes_of((size, elements)) < size
    paired = width // 2

    def through(line, which):
        both = which(line % paired)
        turned = pltpu.roll(both, size, 1)
        return (both, turned) if line < paired else (turned, both)

    def low(n):
        return jnp.where(is_odd, other[n], own[n])

    def high(n):
        return jnp.where(is_odd, own[n], other[n])

    def pack(tile, outs):
        groups = []
        for ih in range(size // SUB):
            for lh in range(width // SUB):
                groups.append(
                    swap_sublanes(
                        [tile(lh * SUB + a)[ih * SUB : (ih + 1) * SUB] for a in range(SUB)]
                    )
                )
        for il in range(SUB):
            turned = jnp.concatenate([rows[il] for rows in groups], axis=0).T
            for n, out in enumerate(outs):
                out[il] = turned[n * size : (n + 1) * size]

    def joined(line):
        left, right = through(line, low)
        both = jnp.where(half, left, right)
        top, bottom = high(paired + line), low(paired + line)
        step = jnp.dot(top[:, :size], both, precision=HIGHEST, preferred_element_type=F32)
        turned = pltpu.roll(bottom, size, 1)
        step = jnp.dot(turned[:, :size], step, precision=HIGHEST, preferred_element_type=F32)
        return jnp.where(half, pltpu.roll(top, size, 1), turned + step)

    first = [
        jnp.where(half, through(line, low)[0], through(line, high)[1]) for line in range(width)
    ]
    pack(lambda line: first[line], (through_low, through_high))
    second = [jnp.where(half, high(paired + line), low(paired + line)) for line in range(width)]
    pack(lambda line: second[line], (reach_high, back_low))
    third = [joined(line) for line in range(width)]
    pack(lambda line: third[line], (back_high, pair))
    for il in range(SUB):
        top = pair[il].astype(BF16)
        message[il] = top
        message[SUB + il] = (pair[il] - top.astype(F32)).astype(BF16)
        before[il] = other[paired + width + il]
        message[2 * SUB + il] = other[paired + width + il].astype(BF16)


def maps(own, other, width):
    size, elements = own.shape[1:]
    shape = jax.ShapeDtypeStruct((SUB, size, elements), F32)
    return pl.pallas_call(
        functools.partial(maps_kernel, width),
        out_shape=(shape,) * 6 + (jax.ShapeDtypeStruct((3 * SUB, size, elements), BF16),),
        scratch_shapes=[pltpu.VMEM((SUB, size, elements), F32)],
        name="line_maps",
        compiler_params=pltpu.CompilerParams(vmem_limit_bytes=10 * MIB),
    )(own, other)


def line_sweeps(width, entries, inv, fwd_steps, bwd_steps, local, ends, source):
    elements = source.shape[1]
    positions = elements // width

    @pl.loop(0, source.shape[0] // SUB)
    def _(n):
        at = pl.multiple_of(n * SUB, SUB)
        source[pl.ds(at, SUB), :] = block_rows([lambda i: inv[at + i]], [entries])

    values = swap_groups(rows_of(source[...]), width)
    for q in range(1, positions):
        values[q] = values[q] + packed_product(lambda il: fwd_steps[q, il], values[q - 1], width)
    ends[:SUB] = values[-1]
    for q in reversed(range(positions - 1)):
        values[q] = values[q] + packed_product(lambda il: bwd_steps[q, il], values[q + 1], width)
    ends[SUB:] = values[0]
    for n, rows in enumerate(swap_groups(values, width)):
        local[SUB * n : SUB * (n + 1), :] = rows


def sweep_kernel(width, right_side, norm, inv, fwd_steps, bwd_steps, local, ends, vector, source):
    vector[...] = right_side[...] / norm[0:1, :]
    rounded = vector[...].astype(BF16).astype(F32)
    line_sweeps(width, rows_of(rounded), inv, fwd_steps, bwd_steps, local, ends, source)


def sweep_shapes(size, elements):
    return (
        jax.ShapeDtypeStruct((size, elements), F32),
        jax.ShapeDtypeStruct((2 * SUB, elements), F32),
        jax.ShapeDtypeStruct((size, elements), F32),
    )


def sweep(right_side, norm, inv, fwd_steps, bwd_steps, width):
    size, elements = right_side.shape
    return pl.pallas_call(
        functools.partial(sweep_kernel, width),
        out_shape=sweep_shapes(size, elements),
        scratch_shapes=[pltpu.VMEM((size, elements), F32)],
        name="line_sweep",
        compiler_params=pltpu.CompilerParams(vmem_limit_bytes=6 * MIB),
    )(right_side, norm, inv, fwd_steps, bwd_steps)


def low_high(own, other):
    is_odd = lax.axis_index("line") % 2 == 1
    mine, theirs = own[...], other[...]
    return is_odd, jnp.where(is_odd, theirs, mine), jnp.where(is_odd, mine, theirs)


def pair_kernel(width, own, other, through_high, reach_high, back_low, ends):
    _, low, high = low_high(own, other)
    passed = high[:SUB] + packed_product(lambda il: through_high[il], low[:SUB], width)
    reached = high[SUB:] + packed_product(lambda il: reach_high[il], low[:SUB], width)
    ends[:SUB] = passed
    ends[SUB:] = low[SUB:] + packed_product(lambda il: back_low[il], reached, width)


def pair_ends(own, other, through_high, reach_high, back_low, width):
    return pl.pallas_call(
        functools.partial(pair_kernel, width),
        out_shape=jax.ShapeDtypeStruct((2 * SUB, own.shape[1]), F32),
        name="line_pair",
        compiler_params=pltpu.CompilerParams(vmem_limit_bytes=4 * MIB),
    )(own, other, through_high, reach_high, back_low)


def correct_kernel(
    width, own, other, pair, far, local, through_low, reach_high, back_high, before, far_maps,
    response, send_list, result, edges, sent,
):
    place = lax.axis_index("line")
    is_upper = place // 2 == 1
    is_odd, low, high = low_high(own, other)
    zero = jnp.zeros(low[:SUB].shape, F32)
    enter = jnp.where(is_upper, far[:SUB], zero)
    crossing = packed_product(
        lambda il: far_maps[il].astype(F32) + far_maps[SUB + il].astype(F32), pair[:SUB], width
    )
    leave = jnp.where(is_upper, zero, far[SUB:] + crossing)
    middle = low[:SUB] + packed_product(lambda il: through_low[il], enter, width)
    meet = (
        high[SUB:]
        + packed_product(lambda il: back_high[il], leave, width)
        + packed_product(lambda il: reach_high[il], middle, width)
    )
    forward = jnp.where(is_odd, middle, enter)
    backward = jnp.where(is_odd, leave, meet)
    entries = spread_groups(forward, width) + spread_groups(backward, width)

    @pl.loop(0, local.shape[0] // SUB)
    def _(n):
        at = pl.multiple_of(n * SUB, SUB)
        result[pl.ds(at, SUB), :] = local[pl.ds(at, SUB), :] + block_rows(
            [lambda i: response[at + i]], [entries]
        )

    first = group_zero(rows_of(result[...]), width)
    back = packed_product(
        lambda il: jnp.where(is_odd, before[il], far_maps[2 * SUB + il].astype(F32)), first, width
    )
    edges[:SUB] = forward + jnp.where(place == 0, zero, back)
    edges[SUB:] = backward
    _, elements = result.shape
    rest = jnp.zeros((1, elements - send_list.shape[0] * send_list.shape[1]), jnp.int32)
    index = jnp.concatenate([send_list[0:1, :], send_list[1:2, :], rest], axis=1)
    index = jnp.broadcast_to(index, result.shape)
    sent[...] = jnp.take_along_axis(result[...], index, axis=1)[:, : sent.shape[1]]


def correct(own, other, pair, far, local, through_low, reach_high, back_high, before, far_maps, response, send_list, width):
    size, elements = local.shape
    return pl.pallas_call(
        functools.partial(correct_kernel, width),
        out_shape=(
            jax.ShapeDtypeStruct((size, elements), F32),
            jax.ShapeDtypeStruct((2 * SUB, elements), F32),
            jax.ShapeDtypeStruct((size, send_list.size), F32),
        ),
        name="line_correct",
        compiler_params=pltpu.CompilerParams(vmem_limit_bytes=10 * MIB),
    )(own, other, pair, far, local, through_low, reach_high, back_high, before, far_maps, response, send_list)


def near_kernel(width, rounded, vector, edges, diag, lower, upper, out):
    size, elements = vector.shape
    lane = lanes_of((SUB, elements))
    center = rows_of(vector[...])
    before = spread_groups(edges[:SUB], width)
    after = spread_groups(edges[SUB:], width)
    earlier = [
        jnp.where(lane < width, edge, pltpu.roll(rows, width, 1))
        for rows, edge in zip(center, before)
    ]
    later = [
        jnp.where(lane >= elements - width, edge, pltpu.roll(rows, elements - width, 1))
        for rows, edge in zip(center, after)
    ]
    if rounded:
        center, earlier, later = (
            [rows.astype(BF16).astype(F32) for rows in each] for each in (center, earlier, later)
        )

    @pl.loop(0, size // SUB)
    def _(n):
        at = pl.multiple_of(n * SUB, SUB)
        out[pl.ds(at, SUB), :] = block_rows(
            [lambda i: diag[at + i], lambda i: lower[at + i], lambda i: upper[at + i]],
            [center, earlier, later],
        )


def near(vector, edges, diag, lower, upper, width, rounded):
    size, elements = vector.shape
    return pl.pallas_call(
        functools.partial(near_kernel, width, rounded),
        out_shape=jax.ShapeDtypeStruct((size, elements), F32),
        name="near_faces",
        compiler_params=pltpu.CompilerParams(vmem_limit_bytes=6 * MIB),
        cost_estimate=pl.CostEstimate(
            flops=6 * size * size * elements, bytes_accessed=6 * size * size * elements, transcendentals=0
        ),
    )(vector, edges, diag, lower, upper)


def pick_faces(rounded, vector, got_a, got_b, face_nbr, picked):
    count, size, elements = picked.shape
    width = got_a.shape[1]
    halo = width // 2
    place, last = lax.axis_index("dom"), lax.axis_size("dom") - 1
    even = place % 2 == 0
    own = vector[...]
    halos = [got_a[...], got_b[...], jnp.zeros((size, elements - 2 * width), F32)]
    halos = jnp.concatenate(halos, axis=1)
    for f in range(count):
        slot = face_nbr[f : f + 1, :]
        left = jnp.logical_and(slot < elements + halo, place > 0)
        right = jnp.logical_and(slot >= elements + halo, slot < elements + width)
        right = jnp.logical_and(right, place < last)
        at_left = slot - elements + jnp.where(even, width, 0)
        at_right = slot - elements + jnp.where(even, 0, width)
        outside = jnp.where(left, at_left, jnp.where(right, at_right, 2 * width))
        at = jnp.broadcast_to(slot, (size, elements))
        outside = jnp.broadcast_to(jnp.clip(outside, 0, elements - 1), (size, elements))
        inner = jnp.take_along_axis(own, jnp.clip(at, 0, elements - 1), axis=1)
        outer = jnp.take_along_axis(halos, outside, axis=1)
        chosen = jnp.where(at < elements, inner, outer)
        if rounded:
            chosen = chosen.astype(BF16).astype(F32)
        picked[f] = chosen


def add_faces(partial, faces, picked, out):
    count, size, _ = picked.shape
    reads = [functools.partial(lambda f, at, i: faces[f, at + i], f) for f in range(count)]

    @pl.loop(0, size // SUB)
    def _(n):
        at = pl.multiple_of(n * SUB, SUB)
        vectors = [rows_of(picked[f]) for f in range(count)]
        out[pl.ds(at, SUB), :] = partial[pl.ds(at, SUB), :] + block_rows(
            [functools.partial(read, at) for read in reads], vectors
        )


def advance_kernel(
    width, rounded, vector, got_a, got_b, face_nbr, partial, faces, inv, fwd_steps, bwd_steps,
    local, ends, out, picked, source,
):
    pick_faces(rounded, vector, got_a, got_b, face_nbr, picked)
    add_faces(partial, faces, picked, out)
    line_sweeps(width, rows_of(out[...]), inv, fwd_steps, bwd_steps, local, ends, source)


def advance(vector, got_a, got_b, face_nbr, partial, faces, inv, fwd_steps, bwd_steps, width, rounded):
    size, elements = vector.shape
    return pl.pallas_call(
        functools.partial(advance_kernel, width, rounded),
        out_shape=sweep_shapes(size, elements),
        scratch_shapes=[
            pltpu.VMEM((faces.shape[0], size, elements), F32),
            pltpu.VMEM((size, elements), F32),
        ],
        name="faces_and_sweep",
        compiler_params=pltpu.CompilerParams(vmem_limit_bytes=10 * MIB),
    )(vector, got_a, got_b, face_nbr, partial, faces, inv, fwd_steps, bwd_steps)


def closing_kernel(rounded, vector, got_a, got_b, face_nbr, partial, faces, *rest):
    basis, (sums, last, picked) = rest[:-3], rest[-3:]
    pick_faces(rounded, vector, got_a, got_b, face_nbr, picked)
    add_faces(partial, faces, picked, last)
    vectors = [rows_of(each[...]) for each in basis] + [rows_of(last[...])]
    lines = []
    for i in range(len(vectors)):
        for j in range(i, len(vectors)):
            lines.append(sum(a * b for a, b in zip(vectors[i], vectors[j])))
    while len(lines) % SUB:
        lines.append(jnp.zeros_like(lines[0]))
    for n in range(0, len(lines), SUB):
        folded = fold_sublanes(lines[n : n + SUB])
        sums[n : n + SUB, :] = jnp.broadcast_to(jnp.sum(folded, axis=1, keepdims=True), folded.shape)


def closing(vector, got_a, got_b, face_nbr, partial, faces, basis, rounded):
    size, elements = vector.shape
    count = len(basis) + 1
    rows = count * (count + 1) // 2
    rows += -rows % SUB
    return pl.pallas_call(
        functools.partial(closing_kernel, rounded),
        out_shape=jax.ShapeDtypeStruct((rows, elements), F32),
        scratch_shapes=[
            pltpu.VMEM((size, elements), F32),
            pltpu.VMEM((faces.shape[0], size, elements), F32),
        ],
        name="faces_and_sums",
        compiler_params=pltpu.CompilerParams(vmem_limit_bytes=8 * MIB),
    )(vector, got_a, got_b, face_nbr, partial, faces, *basis)


def cholesky(entry, count):
    tri = {}
    for i in range(count):
        pivot = entry[i, i]
        for k in range(i):
            pivot = pivot - tri[k, i] * tri[k, i]
        tri[i, i] = jnp.sqrt(pivot)
        for j in range(i + 1, count):
            value = entry[i, j]
            for k in range(i):
                value = value - tri[k, i] * tri[k, j]
            tri[i, j] = value / tri[i, i]
    return tri


def finish_kernel(iters, norm, sums, *rest):
    search, (update, hessenberg, quality) = rest[:iters], rest[iters:]
    count = iters + 1
    entry = {}
    n = 0
    for i in range(count):
        for j in range(i, count):
            entry[i, j] = sums[n : n + 1, :]
            n += 1
    tri = cholesky(entry, count)
    worst = tri[0, 0] * tri[0, 0] / entry[0, 0]
    for i in range(1, count):
        ratio = tri[i, i] * tri[i, i] / entry[i, i]
        worst = jnp.where(ratio > worst, worst, ratio)
    quality[...] = jnp.broadcast_to(worst, quality.shape)
    hess = {}
    for j in range(iters):
        for i in range(j + 2):
            value = tri[i, j + 1]
            for k in range(max(i - 1, 0), j):
                value = value - hess[i, k] * tri[k, j]
            hess[i, j] = value / tri[j, j]
    shape = (count, norm.shape[1])
    row, column = (lax.broadcasted_iota(jnp.int32, shape, axis) for axis in (0, 1))
    table = jnp.zeros(shape, F32)
    for (i, j), value in hess.items():
        table = jnp.where(jnp.logical_and(row == i, column == j), value, table)
    hessenberg[...] = table[:, :iters]
    normal = {}
    for i in range(iters):
        for j in range(i, iters):
            normal[i, j] = sum(hess[k, i] * hess[k, j] for k in range(i + 2))
    factor = cholesky(normal, iters)
    start = norm[0:1, :] * tri[0, 0]
    half = []
    for i in range(iters):
        value = start * hess[0, i]
        for k in range(i):
            value = value - factor[k, i] * half[k]
        half.append(value / factor[i, i])
    coeffs = [None] * iters
    for i in reversed(range(iters)):
        value = half[i]
        for k in range(i + 1, iters):
            value = value - factor[i, k] * coeffs[k]
        coeffs[i] = value / factor[i, i]
    weights = [None] * iters
    for i in reversed(range(iters)):
        value = coeffs[i]
        for k in range(i + 1, iters):
            value = value - tri[i, k] * weights[k]
        weights[i] = value / tri[i, i]
    update[...] = sum(weights[i] * search[i][...] for i in range(iters))


def finish(norm, sums, search):
    iters = len(search)
    size, elements = search[0].shape
    return pl.pallas_call(
        functools.partial(finish_kernel, iters),
        out_shape=(
            jax.ShapeDtypeStruct((size, elements), F32),
            jax.ShapeDtypeStruct((iters + 1, iters), F32),
            jax.ShapeDtypeStruct((1, elements), F32),
        ),
        name="solve_and_update",
        compiler_params=pltpu.CompilerParams(vmem_limit_bytes=2 * MIB),
    )(norm, sums, *search)


def flip(count, bit):
    return [(i, i ^ bit) for i in range(count)]


def neighbour_pairs(count):
    pairs = []
    for i in range(count):
        j = i + 1 if i % 2 else i - 1
        pairs.append((i, j if 0 <= j < count else i))
    return pairs


def sum_over(value, groups):
    axes = ("dom", "line")
    total = lax.axis_size("dom") * lax.axis_size("line")
    for group in groups:
        masks = [0]
        for bit in group:
            masks = masks + [m | bit for m in masks]
        terms = [value] + [lax.ppermute(value, axes, flip(total, m)) for m in masks[1:]]
        while len(terms) > 1:
            terms = [terms[t] + terms[t + 1] for t in range(0, len(terms), 2)]
        value = terms[0]
    return value


def index_bits(limit):
    return [1 << n for n in range((limit - 1).bit_length())]


def set_up(fwd_blocks, bwd_blocks, right_side, width):
    lines, doms = lax.axis_size("line"), lax.axis_size("dom")
    bits = index_bits(doms * lines)
    squares = sum_over(sum_squares(right_side), [bits[1:3]])
    tiles = tile_layouts(fwd_blocks, bwd_blocks)
    fwd_steps, bwd_steps, response, ends = chain_products(tiles, width)
    squares = sum_over(squares, [bits[n : n + 2] for n in range(3, len(bits), 2)])
    other_ends = lax.ppermute(ends, "line", flip(lines, 1))
    norm = jnp.sqrt(sum_over(squares, [bits[:1]]))
    through_low, through_high, reach_high, back_low, back_high, before, message = maps(
        ends, other_ends, width
    )
    far_maps = lax.ppermute(message, "line", flip(lines, 2))
    sweeps = (fwd_steps, bwd_steps)
    pairs = (through_high, reach_high, back_low)
    rest = (through_low, reach_high, back_high, before, far_maps, response)
    return norm, sweeps, pairs, rest


def finish_solve(local, ends_own, pairs, rest, send_list, width):
    lines, doms = lax.axis_size("line"), lax.axis_size("dom")
    ends_other = lax.ppermute(ends_own, "line", flip(lines, 1))
    pair_own = pair_ends(ends_own, ends_other, *pairs, width)
    pair_far = lax.ppermute(pair_own, "line", flip(lines, 2))
    direction, edges, sent = correct(
        ends_own, ends_other, pair_own, pair_far, local, *rest, send_list, width
    )
    got_a = lax.ppermute(sent, "dom", flip(doms, 1))
    got_b = lax.ppermute(sent, "dom", neighbour_pairs(doms))
    return direction, edges, got_a, got_b


def power_basis(
    right_side, diag_blocks, lower_blocks, upper_blocks, face_blocks, face_nbr, send_list,
    inv_blocks, fwd_blocks, bwd_blocks,
):
    width = LINES_DEV
    bits = index_bits(lax.axis_size("dom") * lax.axis_size("line"))
    norm, sweeps, pairs, rest = set_up(fwd_blocks, bwd_blocks, right_side, width)
    local, ends_own, first = sweep(right_side, norm, inv_blocks, *sweeps, width)
    basis = [first]
    search = []
    for iteration in range(ITERS):
        rounded = iteration == 0
        direction, edges, *got = finish_solve(local, ends_own, pairs, rest, send_list, width)
        search.append(direction)
        partial = near(direction, edges, diag_blocks, lower_blocks, upper_blocks, width, rounded)
        given = (direction, *got, face_nbr, partial, face_blocks)
        if iteration + 1 < ITERS:
            local, ends_own, following = advance(*given, inv_blocks, *sweeps, width, rounded)
            basis.append(following)
    groups = [bits[n : n + 2] for n in range(1, len(bits), 2)] + [bits[:1]]
    return finish(norm, sum_over(closing(*given, basis, rounded), groups), search)


def orthogonal_basis(
    right_side, diag_blocks, lower_blocks, upper_blocks, face_blocks, face_nbr, send_list,
    inv_blocks, fwd_blocks, bwd_blocks,
):
    width = LINES_DEV
    _, elements = right_side.shape
    bits = index_bits(lax.axis_size("dom") * lax.axis_size("line"))

    def total(product):
        value = jnp.broadcast_to(jnp.sum(product), (SUB, elements))
        return sum_over(value, [[bit] for bit in bits])

    norm, sweeps, pairs, rest = set_up(fwd_blocks, bwd_blocks, right_side, width)
    local, ends_own, first = sweep(right_side, norm, inv_blocks, *sweeps, width)
    basis = [first]
    search = []
    hess = {}
    for iteration in range(ITERS):
        direction, edges, *got = finish_solve(local, ends_own, pairs, rest, send_list, width)
        search.append(direction)
        partial = near(direction, edges, diag_blocks, lower_blocks, upper_blocks, width, True)
        given = (direction, *got, face_nbr, partial, face_blocks)
        vector = advance(*given, inv_blocks, *sweeps, width, True)[2]
        for column in range(iteration + 1):
            weight = total(vector * basis[column])
            hess[column, iteration] = weight[0, 0]
            vector = vector - weight[0:1] * basis[column]
        height = jnp.sqrt(total(vector * vector))
        hess[iteration + 1, iteration] = height[0, 0]
        if iteration + 1 < ITERS:
            local, ends_own, following = sweep(vector, height, inv_blocks, *sweeps, width)
            basis.append(following)
    zero = jnp.zeros((), F32)
    rows = [[hess.get((i, j), zero) for j in range(ITERS)] for i in range(ITERS + 1)]
    hessenberg = jnp.stack([jnp.stack(row) for row in rows])
    normal = jnp.dot(hessenberg.T, hessenberg, precision=HIGHEST)
    factor = jnp.linalg.cholesky(normal)
    coeffs = jax.scipy.linalg.cho_solve((factor, True), norm[0, 0] * hessenberg[0])
    update = sum(coeffs[n] * search[n] for n in range(ITERS))
    return update, hessenberg


def shards(*arrays):
    update, hessenberg, quality = power_basis(*arrays)
    return lax.cond(
        quality[0, 0] > INDEPENDENT,
        lambda *_: (update, hessenberg),
        orthogonal_basis,
        *arrays,
    )


def solution(mesh):
    in_specs = (
        P(None, ("dom", "line")),
        P(None, None, ("dom", "line")),
        P(None, None, ("dom", "line")),
        P(None, None, ("dom", "line")),
        P(None, None, None, ("dom", "line")),
        P(None, ("dom", "line")),
        P(None, ("dom", "line")),
        P(None, None, ("dom", "line")),
        P(None, None, ("dom", "line")),
        P(None, None, ("dom", "line")),
    )
    out_specs = (P(None, ("dom", "line")), P())
    return jax.shard_map(shards, mesh=mesh, in_specs=in_specs, out_specs=out_specs, check_vma=False)
```

```python
import functools

import jax
import jax.numpy as jnp
from jax import lax
from jax.experimental import pallas as pl
from jax.experimental.pallas import tpu as pltpu
from jax.sharding import PartitionSpec as P


ITERS = 3
LINES_DEV = 16
SUB = 8
MIB = 1 << 20
INDEPENDENT = 0.01
HIGHEST = lax.Precision.HIGHEST
F32 = jnp.float32
BF16 = jnp.bfloat16


def lanes_of(shape):
    return lax.broadcasted_iota(jnp.int32, shape, 1)


def fold_sublanes(parts):
    row = lax.broadcasted_iota(jnp.int32, parts[0].shape, 0)
    step = SUB // 2
    while step:
        mask = (row & step) == 0
        folded = []
        for a in range(step):
            low, high = parts[a], parts[a + step]
            if step == SUB // 2:
                kept = jnp.where(mask, low, high)
                folded.append(kept + pltpu.roll(jnp.where(mask, high, low), step, 0))
            else:
                low = low + pltpu.roll(low, SUB - step, 0)
                high = high + pltpu.roll(high, step, 0)
                folded.append(jnp.where(mask, low, high))
        parts = folded
        step //= 2
    return parts[0]


def choose(arrays, index):
    step = 1
    while len(arrays) > 1:
        clear = (index & step) == 0
        arrays = [jnp.where(clear, arrays[a], arrays[a + 1]) for a in range(0, len(arrays), 2)]
        step *= 2
    return arrays[0]


def spread_groups(packed, width):
    count = packed.shape[1] // width
    group = lanes_of(packed.shape) // width
    moved = [packed] + [pltpu.roll(packed, step * width, 1) for step in range(1, count)]
    return [choose([moved[(g - v) % count] for g in range(count)], group) for v in range(count)]


def swap_groups(arrays, width):
    count = len(arrays)
    group = lanes_of(arrays[0].shape) // width
    moved = [
        [array] + [pltpu.roll(array, step * width, 1) for step in range(1, count)] for array in arrays
    ]
    return [choose([moved[a][(a - q) % count] for a in range(count)], group) for q in range(count)]


def group_zero(arrays, width):
    group = lanes_of(arrays[0].shape) // width
    packed = arrays[0]
    for g in range(1, len(arrays)):
        packed = jnp.where(group == g, pltpu.roll(arrays[g], g * width, 1), packed)
    return packed


def rows_of(array):
    return [array[SUB * g : SUB * (g + 1)] for g in range(array.shape[0] // SUB)]


def packed_product(blocks, packed, width):
    spread = spread_groups(packed, width)
    parts = []
    for il in range(SUB):
        rows = rows_of(blocks(il).astype(F32))
        terms = [rows[g] * spread[g] for g in range(len(rows))]
        while len(terms) > 1:
            terms = [terms[t] + terms[t + 1] for t in range(0, len(terms), 2)]
        parts.append(terms[0])
    return fold_sublanes(parts)


def block_rows(reads, vectors):
    parts = []
    for i in range(SUB):
        total = None
        for read, vector in zip(reads, vectors):
            rows = rows_of(read(i).astype(F32))
            for row, entry in zip(rows, vector):
                term = row * entry
                total = term if total is None else total + term
        parts.append(total)
    return fold_sublanes(parts)


def swap_sublanes(arrays):
    row = lax.broadcasted_iota(jnp.int32, arrays[0].shape, 0)
    arrays = list(arrays)
    step = SUB // 2
    while step:
        clear = (row & step) == 0
        for a in range(SUB):
            if a & step == 0:
                low, high = arrays[a], arrays[a + step]
                arrays[a] = jnp.where(clear, low, pltpu.roll(high, step, 0))
                arrays[a + step] = jnp.where(clear, pltpu.roll(low, SUB - step, 0), high)
        step //= 2
    return arrays


def tiles_kernel(fwd, bwd, tiles):
    size, _, elements = fwd.shape

    @pl.loop(0, size // SUB)
    def _(n):
        turned = []
        for il in range(SUB):
            both = jnp.concatenate(
                [fwd[n * SUB + il].astype(F32), bwd[n * SUB + il].astype(F32)], axis=0
            )
            turned.append(-both.T)
        for g in range(elements // SUB):
            rows = swap_sublanes([t[g * SUB : (g + 1) * SUB] for t in turned])
            for a in range(SUB):
                tiles[pl.ds((g * SUB + a) * size + n * SUB, SUB), :] = rows[a]


def tile_layouts(fwd, bwd):
    size, _, elements = fwd.shape
    return pl.pallas_call(
        tiles_kernel,
        out_shape=jax.ShapeDtypeStruct((elements * size, 2 * size), F32),
        name="tile_layouts",
        compiler_params=pltpu.CompilerParams(vmem_limit_bytes=10 * MIB),
        cost_estimate=pl.CostEstimate(flops=4000000, bytes_accessed=10 * MIB, transcendentals=0),
    )(fwd, bwd)


def squares_kernel(vector, squares):
    total = sum(rows * rows for rows in rows_of(vector[...]))
    total = jnp.sum(jnp.sum(total, axis=1, keepdims=True), axis=0, keepdims=True)
    squares[...] = jnp.broadcast_to(total, squares.shape)


def sum_squares(vector):
    return pl.pallas_call(
        squares_kernel,
        out_shape=jax.ShapeDtypeStruct((SUB, vector.shape[1]), F32),
        name="sum_squares",
        compiler_params=pltpu.CompilerParams(vmem_limit_bytes=MIB),
        cost_estimate=pl.CostEstimate(flops=10**10, bytes_accessed=64 * MIB, transcendentals=0),
    )(vector)


def chain_kernel(width, size, tiles, fwd_steps, bwd_steps, chain, ends):
    elements = tiles.shape[0] // size
    positions = elements // width
    half = lanes_of((size, elements)) < size

    def tile(e):
        return tiles[pl.ds(pl.multiple_of(e * size, size), size), :]

    def split(value):
        high = value.astype(BF16)
        return high, (value - high.astype(F32)).astype(BF16)

    zeros = jnp.zeros((size, 2 * elements), BF16)
    for line in range(width):
        first = tile(line)
        chain[pl.ds(line * size, size), :] = jnp.where(half, first, pltpu.roll(first, size, 1))

    def form_steps(q):
        groups = []
        for ih in range(size // SUB):
            for lh in range(width // SUB):
                start = (q * width + lh * SUB) * size + ih * SUB
                groups.append(
                    swap_sublanes([tiles[pl.ds(start + a * size, SUB), :] for a in range(SUB)])
                )
        for il in range(SUB):
            turned = jnp.concatenate([rows[il] for rows in groups], axis=0).T
            fwd_steps[q, il] = turned[:size].astype(BF16)
            bwd_steps[q, il] = turned[size:].astype(BF16)

    @pl.loop(1, positions)
    def _(q):
        form_steps(q)
        for line in range(width):
            e = q * width + line
            before = chain[pl.ds(pl.multiple_of((e - width) * size, size), size), :]
            high, low = split(before)
            right = jnp.where(half, high, low)
            out = jnp.dot(tile(e)[:, :size].astype(BF16), right, preferred_element_type=F32)
            chain[pl.ds(pl.multiple_of(e * size, size), size), :] = out + pltpu.roll(out, size, 1)

    form_steps(0)
    last = positions - 1
    paired = width // 2
    for line in range(paired):
        e = last * width + line
        one = chain[pl.ds(e * size, size), :]
        two = chain[pl.ds((e + paired) * size, size), :]
        ends[line] = jnp.where(half, one, two)
    for line in range(width):
        e = last * width + line
        chain[pl.ds(e * size, size), :] = jnp.where(half, chain[pl.ds(e * size, size), :], tile(e))

    @pl.loop(0, last)
    def _(n):
        q = last - 1 - n
        for line in range(width):
            e = q * width + line
            after = chain[pl.ds(pl.multiple_of((e + width) * size, size), size), :]
            high, low = split(after)
            right = jnp.concatenate([zeros, jnp.concatenate([high, low], axis=1)], axis=0)
            out = jnp.dot(tile(e).astype(BF16), right, preferred_element_type=F32)
            own = chain[pl.ds(pl.multiple_of(e * size, size), size), :]
            chain[pl.ds(pl.multiple_of(e * size, size), size), :] = (
                jnp.where(half, own, 0.0) + out[:, :elements] + out[:, elements:]
            )

    for line in range(width):
        ends[paired + line] = chain[pl.ds(line * size, size), :]
    ends[paired + width :] = bwd_steps[last].astype(F32)


def response_kernel(chain, response):
    size, _, elements = response.shape

    @pl.loop(0, size // SUB)
    def _(n):
        groups = []
        for g in range(elements // SUB):
            groups.append(
                swap_sublanes(
                    [chain[pl.ds((g * SUB + a) * size + n * SUB, SUB), :] for a in range(SUB)]
                )
            )
        for il in range(SUB):
            response[n * SUB + il] = jnp.concatenate([rows[il] for rows in groups], axis=0).T


def response_layout(chain, size):
    elements = chain.shape[0] // size
    return pl.pallas_call(
        response_kernel,
        out_shape=jax.ShapeDtypeStruct((size, 2 * size, elements), F32),
        name="response_layout",
        compiler_params=pltpu.CompilerParams(vmem_limit_bytes=12 * MIB),
        cost_estimate=pl.CostEstimate(flops=4000000, bytes_accessed=8 * MIB, transcendentals=0),
    )(chain)


def chain_products(tiles, width):
    elements = tiles.shape[1]
    size = tiles.shape[0] // elements
    steps = jax.ShapeDtypeStruct((elements // width, SUB, size, elements), BF16)
    return pl.pallas_call(
        functools.partial(chain_kernel, width, size),
        out_shape=(
            steps,
            steps,
            jax.ShapeDtypeStruct((elements * size, 2 * size), F32),
            jax.ShapeDtypeStruct((width + width // 2 + SUB, size, elements), F32),
        ),
        name="chain_products",
        compiler_params=pltpu.CompilerParams(vmem_limit_bytes=16 * MIB),
        cost_estimate=pl.CostEstimate(flops=40000000, bytes_accessed=12 * MIB, transcendentals=0),
    )(tiles)


def maps_kernel(
    width, own, other, through_low, through_high, reach_high, back_low, back_high, before, message, pair
):
    size = own.shape[1]
    elements = own.shape[2]
    is_odd = lax.axis_index("line") % 2 == 1
    half = lanes_of((size, elements)) < size
    paired = width // 2

    def through(line, which):
        both = which(line % paired)
        turned = pltpu.roll(both, size, 1)
        return (both, turned) if line < paired else (turned, both)

    def low(n):
        return jnp.where(is_odd, other[n], own[n])

    def high(n):
        return jnp.where(is_odd, own[n], other[n])

    def pack(tile, outs):
        groups = []
        for ih in range(size // SUB):
            for lh in range(width // SUB):
                groups.append(
                    swap_sublanes(
                        [tile(lh * SUB + a)[ih * SUB : (ih + 1) * SUB] for a in range(SUB)]
                    )
                )
        for il in range(SUB):
            turned = jnp.concatenate([rows[il] for rows in groups], axis=0).T
            for n, out in enumerate(outs):
                out[il] = turned[n * size : (n + 1) * size]

    def joined(line):
        left, right = through(line, low)
        both = jnp.where(half, left, right)
        top, bottom = high(paired + line), low(paired + line)
        step = jnp.dot(top[:, :size], both, precision=HIGHEST, preferred_element_type=F32)
        turned = pltpu.roll(bottom, size, 1)
        step = jnp.dot(turned[:, :size], step, precision=HIGHEST, preferred_element_type=F32)
        return jnp.where(half, pltpu.roll(top, size, 1), turned + step)

    first = [
        jnp.where(half, through(line, low)[0], through(line, high)[1]) for line in range(width)
    ]
    pack(lambda line: first[line], (through_low, through_high))
    second = [jnp.where(half, high(paired + line), low(paired + line)) for line in range(width)]
    pack(lambda line: second[line], (reach_high, back_low))
    third = [joined(line) for line in range(width)]
    pack(lambda line: third[line], (back_high, pair))
    for il in range(SUB):
        top = pair[il].astype(BF16)
        message[il] = top
        message[SUB + il] = (pair[il] - top.astype(F32)).astype(BF16)
        before[il] = other[paired + width + il]
        message[2 * SUB + il] = other[paired + width + il].astype(BF16)


def maps(own, other, width):
    size, elements = own.shape[1:]
    shape = jax.ShapeDtypeStruct((SUB, size, elements), F32)
    return pl.pallas_call(
        functools.partial(maps_kernel, width),
        out_shape=(shape,) * 6 + (jax.ShapeDtypeStruct((3 * SUB, size, elements), BF16),),
        scratch_shapes=[pltpu.VMEM((SUB, size, elements), F32)],
        name="line_maps",
        compiler_params=pltpu.CompilerParams(vmem_limit_bytes=10 * MIB),
    )(own, other)


def line_sweeps(width, entries, inv, fwd_steps, bwd_steps, local, ends, source):
    elements = source.shape[1]
    positions = elements // width

    @pl.loop(0, source.shape[0] // SUB)
    def _(n):
        at = pl.multiple_of(n * SUB, SUB)
        source[pl.ds(at, SUB), :] = block_rows([lambda i: inv[at + i]], [entries])

    values = swap_groups(rows_of(source[...]), width)
    for q in range(1, positions):
        values[q] = values[q] + packed_product(lambda il: fwd_steps[q, il], values[q - 1], width)
    ends[:SUB] = values[-1]
    for q in reversed(range(positions - 1)):
        values[q] = values[q] + packed_product(lambda il: bwd_steps[q, il], values[q + 1], width)
    ends[SUB:] = values[0]
    for n, rows in enumerate(swap_groups(values, width)):
        local[SUB * n : SUB * (n + 1), :] = rows


def sweep_kernel(width, right_side, norm, inv, fwd_steps, bwd_steps, local, ends, vector, source):
    vector[...] = right_side[...] / norm[0:1, :]
    rounded = vector[...].astype(BF16).astype(F32)
    line_sweeps(width, rows_of(rounded), inv, fwd_steps, bwd_steps, local, ends, source)


def sweep_shapes(size, elements):
    return (
        jax.ShapeDtypeStruct((size, elements), F32),
        jax.ShapeDtypeStruct((2 * SUB, elements), F32),
        jax.ShapeDtypeStruct((size, elements), F32),
    )


def sweep(right_side, norm, inv, fwd_steps, bwd_steps, width):
    size, elements = right_side.shape
    return pl.pallas_call(
        functools.partial(sweep_kernel, width),
        out_shape=sweep_shapes(size, elements),
        scratch_shapes=[pltpu.VMEM((size, elements), F32)],
        name="line_sweep",
        compiler_params=pltpu.CompilerParams(vmem_limit_bytes=6 * MIB),
    )(right_side, norm, inv, fwd_steps, bwd_steps)


def low_high(own, other):
    is_odd = lax.axis_index("line") % 2 == 1
    mine, theirs = own[...], other[...]
    return is_odd, jnp.where(is_odd, theirs, mine), jnp.where(is_odd, mine, theirs)


def pair_kernel(width, own, other, through_high, reach_high, back_low, ends):
    _, low, high = low_high(own, other)
    passed = high[:SUB] + packed_product(lambda il: through_high[il], low[:SUB], width)
    reached = high[SUB:] + packed_product(lambda il: reach_high[il], low[:SUB], width)
    ends[:SUB] = passed
    ends[SUB:] = low[SUB:] + packed_product(lambda il: back_low[il], reached, width)


def pair_ends(own, other, through_high, reach_high, back_low, width):
    return pl.pallas_call(
        functools.partial(pair_kernel, width),
        out_shape=jax.ShapeDtypeStruct((2 * SUB, own.shape[1]), F32),
        name="line_pair",
        compiler_params=pltpu.CompilerParams(vmem_limit_bytes=4 * MIB),
    )(own, other, through_high, reach_high, back_low)


def correct_kernel(
    width, own, other, pair, far, local, through_low, reach_high, back_high, before, far_maps,
    response, send_list, result, edges, sent,
):
    place = lax.axis_index("line")
    is_upper = place // 2 == 1
    is_odd, low, high = low_high(own, other)
    zero = jnp.zeros(low[:SUB].shape, F32)
    enter = jnp.where(is_upper, far[:SUB], zero)
    crossing = packed_product(
        lambda il: far_maps[il].astype(F32) + far_maps[SUB + il].astype(F32), pair[:SUB], width
    )
    leave = jnp.where(is_upper, zero, far[SUB:] + crossing)
    middle = low[:SUB] + packed_product(lambda il: through_low[il], enter, width)
    meet = (
        high[SUB:]
        + packed_product(lambda il: back_high[il], leave, width)
        + packed_product(lambda il: reach_high[il], middle, width)
    )
    forward = jnp.where(is_odd, middle, enter)
    backward = jnp.where(is_odd, leave, meet)
    entries = spread_groups(forward, width) + spread_groups(backward, width)

    @pl.loop(0, local.shape[0] // SUB)
    def _(n):
        at = pl.multiple_of(n * SUB, SUB)
        result[pl.ds(at, SUB), :] = local[pl.ds(at, SUB), :] + block_rows(
            [lambda i: response[at + i]], [entries]
        )

    first = group_zero(rows_of(result[...]), width)
    back = packed_product(
        lambda il: jnp.where(is_odd, before[il], far_maps[2 * SUB + il].astype(F32)), first, width
    )
    edges[:SUB] = forward + jnp.where(place == 0, zero, back)
    edges[SUB:] = backward
    _, elements = result.shape
    rest = jnp.zeros((1, elements - send_list.shape[0] * send_list.shape[1]), jnp.int32)
    index = jnp.concatenate([send_list[0:1, :], send_list[1:2, :], rest], axis=1)
    index = jnp.broadcast_to(index, result.shape)
    sent[...] = jnp.take_along_axis(result[...], index, axis=1)[:, : sent.shape[1]]


def correct(own, other, pair, far, local, through_low, reach_high, back_high, before, far_maps, response, send_list, width):
    size, elements = local.shape
    return pl.pallas_call(
        functools.partial(correct_kernel, width),
        out_shape=(
            jax.ShapeDtypeStruct((size, elements), F32),
            jax.ShapeDtypeStruct((2 * SUB, elements), F32),
            jax.ShapeDtypeStruct((size, send_list.size), F32),
        ),
        name="line_correct",
        compiler_params=pltpu.CompilerParams(vmem_limit_bytes=10 * MIB),
    )(own, other, pair, far, local, through_low, reach_high, back_high, before, far_maps, response, send_list)


def near_kernel(width, rounded, vector, edges, diag, lower, upper, out):
    size, elements = vector.shape
    lane = lanes_of((SUB, elements))
    center = rows_of(vector[...])
    before = spread_groups(edges[:SUB], width)
    after = spread_groups(edges[SUB:], width)
    earlier = [
        jnp.where(lane < width, edge, pltpu.roll(rows, width, 1))
        for rows, edge in zip(center, before)
    ]
    later = [
        jnp.where(lane >= elements - width, edge, pltpu.roll(rows, elements - width, 1))
        for rows, edge in zip(center, after)
    ]
    if rounded:
        center, earlier, later = (
            [rows.astype(BF16).astype(F32) for rows in each] for each in (center, earlier, later)
        )

    @pl.loop(0, size // SUB)
    def _(n):
        at = pl.multiple_of(n * SUB, SUB)
        out[pl.ds(at, SUB), :] = block_rows(
            [lambda i: diag[at + i], lambda i: lower[at + i], lambda i: upper[at + i]],
            [center, earlier, later],
        )


def near(vector, edges, diag, lower, upper, width, rounded):
    size, elements = vector.shape
    return pl.pallas_call(
        functools.partial(near_kernel, width, rounded),
        out_shape=jax.ShapeDtypeStruct((size, elements), F32),
        name="near_faces",
        compiler_params=pltpu.CompilerParams(vmem_limit_bytes=6 * MIB),
        cost_estimate=pl.CostEstimate(
            flops=6 * size * size * elements, bytes_accessed=6 * size * size * elements, transcendentals=0
        ),
    )(vector, edges, diag, lower, upper)


def pick_faces(rounded, vector, got_a, got_b, face_nbr, picked):
    count, size, elements = picked.shape
    width = got_a.shape[1]
    halo = width // 2
    place, last = lax.axis_index("dom"), lax.axis_size("dom") - 1
    even = place % 2 == 0
    own = vector[...]
    halos = [got_a[...], got_b[...], jnp.zeros((size, elements - 2 * width), F32)]
    halos = jnp.concatenate(halos, axis=1)
    for f in range(count):
        slot = face_nbr[f : f + 1, :]
        left = jnp.logical_and(slot < elements + halo, place > 0)
        right = jnp.logical_and(slot >= elements + halo, slot < elements + width)
        right = jnp.logical_and(right, place < last)
        at_left = slot - elements + jnp.where(even, width, 0)
        at_right = slot - elements + jnp.where(even, 0, width)
        outside = jnp.where(left, at_left, jnp.where(right, at_right, 2 * width))
        at = jnp.broadcast_to(slot, (size, elements))
        outside = jnp.broadcast_to(jnp.clip(outside, 0, elements - 1), (size, elements))
        inner = jnp.take_along_axis(own, jnp.clip(at, 0, elements - 1), axis=1)
        outer = jnp.take_along_axis(halos, outside, axis=1)
        chosen = jnp.where(at < elements, inner, outer)
        if rounded:
            chosen = chosen.astype(BF16).astype(F32)
        picked[f] = chosen


def add_faces(partial, faces, picked, out):
    count, size, _ = picked.shape
    reads = [functools.partial(lambda f, at, i: faces[f, at + i], f) for f in range(count)]

    @pl.loop(0, size // SUB)
    def _(n):
        at = pl.multiple_of(n * SUB, SUB)
        vectors = [rows_of(picked[f]) for f in range(count)]
        out[pl.ds(at, SUB), :] = partial[pl.ds(at, SUB), :] + block_rows(
            [functools.partial(read, at) for read in reads], vectors
        )


def advance_kernel(
    width, rounded, vector, got_a, got_b, face_nbr, partial, faces, inv, fwd_steps, bwd_steps,
    local, ends, out, picked, source,
):
    pick_faces(rounded, vector, got_a, got_b, face_nbr, picked)
    add_faces(partial, faces, picked, out)
    line_sweeps(width, rows_of(out[...]), inv, fwd_steps, bwd_steps, local, ends, source)


def advance(vector, got_a, got_b, face_nbr, partial, faces, inv, fwd_steps, bwd_steps, width, rounded):
    size, elements = vector.shape
    return pl.pallas_call(
        functools.partial(advance_kernel, width, rounded),
        out_shape=sweep_shapes(size, elements),
        scratch_shapes=[
            pltpu.VMEM((faces.shape[0], size, elements), F32),
            pltpu.VMEM((size, elements), F32),
        ],
        name="faces_and_sweep",
        compiler_params=pltpu.CompilerParams(vmem_limit_bytes=10 * MIB),
    )(vector, got_a, got_b, face_nbr, partial, faces, inv, fwd_steps, bwd_steps)


def closing_kernel(rounded, vector, got_a, got_b, face_nbr, partial, faces, *rest):
    basis, (sums, last, picked) = rest[:-3], rest[-3:]
    pick_faces(rounded, vector, got_a, got_b, face_nbr, picked)
    add_faces(partial, faces, picked, last)
    vectors = [rows_of(each[...]) for each in basis] + [rows_of(last[...])]
    lines = []
    for i in range(len(vectors)):
        for j in range(i, len(vectors)):
            lines.append(sum(a * b for a, b in zip(vectors[i], vectors[j])))
    while len(lines) % SUB:
        lines.append(jnp.zeros_like(lines[0]))
    for n in range(0, len(lines), SUB):
        folded = fold_sublanes(lines[n : n + SUB])
        sums[n : n + SUB, :] = jnp.broadcast_to(jnp.sum(folded, axis=1, keepdims=True), folded.shape)


def closing(vector, got_a, got_b, face_nbr, partial, faces, basis, rounded):
    size, elements = vector.shape
    count = len(basis) + 1
    rows = count * (count + 1) // 2
    rows += -rows % SUB
    return pl.pallas_call(
        functools.partial(closing_kernel, rounded),
        out_shape=jax.ShapeDtypeStruct((rows, elements), F32),
        scratch_shapes=[
            pltpu.VMEM((size, elements), F32),
            pltpu.VMEM((faces.shape[0], size, elements), F32),
        ],
        name="faces_and_sums",
        compiler_params=pltpu.CompilerParams(vmem_limit_bytes=8 * MIB),
    )(vector, got_a, got_b, face_nbr, partial, faces, *basis)


def cholesky(entry, count):
    tri = {}
    for i in range(count):
        pivot = entry[i, i]
        for k in range(i):
            pivot = pivot - tri[k, i] * tri[k, i]
        tri[i, i] = jnp.sqrt(pivot)
        for j in range(i + 1, count):
            value = entry[i, j]
            for k in range(i):
                value = value - tri[k, i] * tri[k, j]
            tri[i, j] = value / tri[i, i]
    return tri


def finish_kernel(iters, norm, sums, *rest):
    search, (update, hessenberg, quality) = rest[:iters], rest[iters:]
    count = iters + 1
    entry = {}
    n = 0
    for i in range(count):
        for j in range(i, count):
            entry[i, j] = sums[n : n + 1, :]
            n += 1
    tri = cholesky(entry, count)
    worst = tri[0, 0] * tri[0, 0] / entry[0, 0]
    for i in range(1, count):
        ratio = tri[i, i] * tri[i, i] / entry[i, i]
        worst = jnp.where(ratio > worst, worst, ratio)
    quality[...] = jnp.broadcast_to(worst, quality.shape)
    hess = {}
    for j in range(iters):
        for i in range(j + 2):
            value = tri[i, j + 1]
            for k in range(max(i - 1, 0), j):
                value = value - hess[i, k] * tri[k, j]
            hess[i, j] = value / tri[j, j]
    shape = (count, norm.shape[1])
    row, column = (lax.broadcasted_iota(jnp.int32, shape, axis) for axis in (0, 1))
    table = jnp.zeros(shape, F32)
    for (i, j), value in hess.items():
        table = jnp.where(jnp.logical_and(row == i, column == j), value, table)
    hessenberg[...] = table[:, :iters]
    normal = {}
    for i in range(iters):
        for j in range(i, iters):
            normal[i, j] = sum(hess[k, i] * hess[k, j] for k in range(i + 2))
    factor = cholesky(normal, iters)
    start = norm[0:1, :] * tri[0, 0]
    half = []
    for i in range(iters):
        value = start * hess[0, i]
        for k in range(i):
            value = value - factor[k, i] * half[k]
        half.append(value / factor[i, i])
    coeffs = [None] * iters
    for i in reversed(range(iters)):
        value = half[i]
        for k in range(i + 1, iters):
            value = value - factor[i, k] * coeffs[k]
        coeffs[i] = value / factor[i, i]
    weights = [None] * iters
    for i in reversed(range(iters)):
        value = coeffs[i]
        for k in range(i + 1, iters):
            value = value - tri[i, k] * weights[k]
        weights[i] = value / tri[i, i]
    update[...] = sum(weights[i] * search[i][...] for i in range(iters))


def finish(norm, sums, search):
    iters = len(search)
    size, elements = search[0].shape
    return pl.pallas_call(
        functools.partial(finish_kernel, iters),
        out_shape=(
            jax.ShapeDtypeStruct((size, elements), F32),
            jax.ShapeDtypeStruct((iters + 1, iters), F32),
            jax.ShapeDtypeStruct((1, elements), F32),
        ),
        name="solve_and_update",
        compiler_params=pltpu.CompilerParams(vmem_limit_bytes=2 * MIB),
    )(norm, sums, *search)


def flip(count, bit):
    return [(i, i ^ bit) for i in range(count)]


def neighbour_pairs(count):
    pairs = []
    for i in range(count):
        j = i + 1 if i % 2 else i - 1
        pairs.append((i, j if 0 <= j < count else i))
    return pairs


def sum_over(value, groups):
    axes = ("dom", "line")
    total = lax.axis_size("dom") * lax.axis_size("line")
    for group in groups:
        masks = [0]
        for bit in group:
            masks = masks + [m | bit for m in masks]
        terms = [value] + [lax.ppermute(value, axes, flip(total, m)) for m in masks[1:]]
        while len(terms) > 1:
            terms = [terms[t] + terms[t + 1] for t in range(0, len(terms), 2)]
        value = terms[0]
    return value


def index_bits(limit):
    return [1 << n for n in range((limit - 1).bit_length())]


def set_up(fwd_blocks, bwd_blocks, right_side, width):
    lines, doms = lax.axis_size("line"), lax.axis_size("dom")
    bits = index_bits(doms * lines)
    squares = sum_over(sum_squares(right_side), [bits[1:3]])
    tiles = tile_layouts(fwd_blocks, bwd_blocks)
    fwd_steps, bwd_steps, chain, ends = chain_products(tiles, width)
    squares = sum_over(squares, [bits[n : n + 2] for n in range(3, len(bits), 2)])
    other_ends = lax.ppermute(ends, "line", flip(lines, 1))
    norm = jnp.sqrt(sum_over(squares, [bits[:1]]))
    through_low, through_high, reach_high, back_low, back_high, before, message = maps(
        ends, other_ends, width
    )
    far_maps = lax.ppermute(message, "line", flip(lines, 2))
    response = response_layout(chain, right_side.shape[0])
    sweeps = (fwd_steps, bwd_steps)
    pairs = (through_high, reach_high, back_low)
    rest = (through_low, reach_high, back_high, before, far_maps, response)
    return norm, sweeps, pairs, rest


def finish_solve(local, ends_own, pairs, rest, send_list, width):
    lines, doms = lax.axis_size("line"), lax.axis_size("dom")
    ends_other = lax.ppermute(ends_own, "line", flip(lines, 1))
    pair_own = pair_ends(ends_own, ends_other, *pairs, width)
    pair_far = lax.ppermute(pair_own, "line", flip(lines, 2))
    direction, edges, sent = correct(
        ends_own, ends_other, pair_own, pair_far, local, *rest, send_list, width
    )
    got_a = lax.ppermute(sent, "dom", flip(doms, 1))
    got_b = lax.ppermute(sent, "dom", neighbour_pairs(doms))
    return direction, edges, got_a, got_b


def power_basis(
    right_side, diag_blocks, lower_blocks, upper_blocks, face_blocks, face_nbr, send_list,
    inv_blocks, fwd_blocks, bwd_blocks,
):
    width = LINES_DEV
    bits = index_bits(lax.axis_size("dom") * lax.axis_size("line"))
    norm, sweeps, pairs, rest = set_up(fwd_blocks, bwd_blocks, right_side, width)
    local, ends_own, first = sweep(right_side, norm, inv_blocks, *sweeps, width)
    basis = [first]
    search = []
    for iteration in range(ITERS):
        rounded = iteration == 0
        direction, edges, *got = finish_solve(local, ends_own, pairs, rest, send_list, width)
        search.append(direction)
        partial = near(direction, edges, diag_blocks, lower_blocks, upper_blocks, width, rounded)
        given = (direction, *got, face_nbr, partial, face_blocks)
        if iteration + 1 < ITERS:
            local, ends_own, following = advance(*given, inv_blocks, *sweeps, width, rounded)
            basis.append(following)
    groups = [bits[n : n + 2] for n in range(1, len(bits), 2)] + [bits[:1]]
    return finish(norm, sum_over(closing(*given, basis, rounded), groups), search)


def orthogonal_basis(
    right_side, diag_blocks, lower_blocks, upper_blocks, face_blocks, face_nbr, send_list,
    inv_blocks, fwd_blocks, bwd_blocks,
):
    width = LINES_DEV
    _, elements = right_side.shape
    bits = index_bits(lax.axis_size("dom") * lax.axis_size("line"))

    def total(product):
        value = jnp.broadcast_to(jnp.sum(product), (SUB, elements))
        return sum_over(value, [[bit] for bit in bits])

    norm, sweeps, pairs, rest = set_up(fwd_blocks, bwd_blocks, right_side, width)
    local, ends_own, first = sweep(right_side, norm, inv_blocks, *sweeps, width)
    basis = [first]
    search = []
    hess = {}
    for iteration in range(ITERS):
        direction, edges, *got = finish_solve(local, ends_own, pairs, rest, send_list, width)
        search.append(direction)
        partial = near(direction, edges, diag_blocks, lower_blocks, upper_blocks, width, True)
        given = (direction, *got, face_nbr, partial, face_blocks)
        vector = advance(*given, inv_blocks, *sweeps, width, True)[2]
        for column in range(iteration + 1):
            weight = total(vector * basis[column])
            hess[column, iteration] = weight[0, 0]
            vector = vector - weight[0:1] * basis[column]
        height = jnp.sqrt(total(vector * vector))
        hess[iteration + 1, iteration] = height[0, 0]
        if iteration + 1 < ITERS:
            local, ends_own, following = sweep(vector, height, inv_blocks, *sweeps, width)
            basis.append(following)
    zero = jnp.zeros((), F32)
    rows = [[hess.get((i, j), zero) for j in range(ITERS)] for i in range(ITERS + 1)]
    hessenberg = jnp.stack([jnp.stack(row) for row in rows])
    normal = jnp.dot(hessenberg.T, hessenberg, precision=HIGHEST)
    factor = jnp.linalg.cholesky(normal)
    coeffs = jax.scipy.linalg.cho_solve((factor, True), norm[0, 0] * hessenberg[0])
    update = sum(coeffs[n] * search[n] for n in range(ITERS))
    return update, hessenberg


def shards(*arrays):
    update, hessenberg, quality = power_basis(*arrays)
    return lax.cond(
        quality[0, 0] > INDEPENDENT,
        lambda *_: (update, hessenberg),
        orthogonal_basis,
        *arrays,
    )


def solution(mesh):
    in_specs = (
        P(None, ("dom", "line")),
        P(None, None, ("dom", "line")),
        P(None, None, ("dom", "line")),
        P(None, None, ("dom", "line")),
        P(None, None, None, ("dom", "line")),
        P(None, ("dom", "line")),
        P(None, ("dom", "line")),
        P(None, None, ("dom", "line")),
        P(None, None, ("dom", "line")),
        P(None, None, ("dom", "line")),
    )
    out_specs = (P(None, ("dom", "line")), P())
    return jax.shard_map(shards, mesh=mesh, in_specs=in_specs, out_specs=out_specs, check_vma=False)
```
